512 devices in a mesh: dp: 4 (over z_hi), pipe: 4 (over z_lo, core), sg: 32 (over y, x).
Axes of the slice: x: 4, y: 8, z: 8 (z_hi: 4, z_lo: 2; z = z_hi * 2 + z_lo), core: 2. Of those that a mesh axis runs over, the one named last changes fastest.
Arguments:
- inputs: bfloat16 [4, 4, 32, 16, 16, 256], P('pipe', 'dp', 'sg'), may hold values from -6 to 6
- cotangent: bfloat16 [4, 4, 32, 16, 16, 256], P('pipe', 'dp', 'sg'), may hold values from -6 to 6
- w_in: bfloat16 [4, 256, 256], P('pipe'), may hold values from -0.375 to 0.375
- w_out: bfloat16 [4, 256, 256], P('pipe'), may hold values from -0.375 to 0.375
- w_group: bfloat16 [4, 3, 3, 3, 8, 256], P('pipe'), may hold values from -0.4375 to 0.4375
Outputs:
- section_grad: bfloat16 [4, 4, 32, 16, 16, 256], P('pipe', 'dp', 'sg')
- grad_in: float32 [4, 256, 256], P('pipe', ('dp', 'sg'))
- grad_out: float32 [4, 256, 256], P('pipe', ('dp', 'sg'))
- grad_group: float32 [4, 3, 3, 3, 8, 256], P('pipe', None, None, None, None, 'sg')
The draws below stay inside these ranges and needn't reach their ends.
All inputs are finite; a program needn't handle non-finite values.
Results may differ from the reference program's by a relative error of at most 0.0065.
Values may be sent and summed in bfloat16 or wider, within the bound.
No kernel may reach another device: no remote copies, remote signals or barrier semaphores. Data moves between devices by JAX's collectives and lax.ppermute only.
A program may use at most 64 MiB of HBM per device.

```python
import jax
import jax.numpy as jnp
from jax import lax

C = 256
GW = 8
SIDE = 16
DEPTH = 32
BATCH = 4
SECTIONS = 4
N_PIPE = 4


def level_of(rng, shape, pieces, low, top_value):
    factor_of = 1.0
    for axis_at, blocks in pieces:
        steps = jax.random.uniform(jax.random.fold_in(jax.random.fold_in(rng, 6), axis_at), (blocks,), jnp.float32, low / len(pieces), top_value / len(pieces))
        factor_of = factor_of * jnp.repeat(jnp.exp(steps), shape[axis_at] // blocks).reshape((-1,) + (1,) * (len(shape) - 1 - axis_at))
    return factor_of


def noise(stream_key, extent, spread, most, shards=(), dtype=jnp.bfloat16):
    gain = level_of(stream_key, extent, shards, -0.22, 0.18) if shards else 1.0
    entries = jax.random.normal(stream_key, extent, jnp.float32) * spread * gain
    return jnp.minimum(jnp.maximum(entries, -most), most).astype(dtype)


def setup_inputs(seed: int = 0) -> dict:
    key_list = jax.random.split(jax.random.key(seed), 6)
    inputs = noise(key_list[0], (SECTIONS, BATCH, DEPTH, SIDE, SIDE, C), 1.0, 6.0, ((0, 4), (1, 4), (2, 32)))
    cotangent = noise(key_list[1], (SECTIONS, BATCH, DEPTH, SIDE, SIDE, C), 1.0, 6.0, ((0, 4), (1, 4), (2, 32)))
    w_in = noise(key_list[2], (SECTIONS, C, C), C ** -0.5, 0.375, ((0, 4),))
    w_out = noise(key_list[3], (SECTIONS, C, C), C ** -0.5, 0.375, ((0, 4),))
    w_group = noise(key_list[4], (SECTIONS, 3, 3, 3, GW, C), (27 * GW) ** -0.5, 0.4375, ((0, 4),))
    return {"inputs": inputs, "cotangent": cotangent, "w_in": w_in, "w_out": w_out, "w_group": w_group}


def silu_slope(value):
    sigmoid_value = jax.nn.sigmoid(value)
    return sigmoid_value * (1.0 + value * (1.0 - sigmoid_value))

def group_conv(padded, kernel, groups):
    return lax.conv_general_dilated(padded, kernel, (1, 1, 1), ((0, 0), (1, 1), (1, 1)), dimension_numbers=('NDHWC', 'DHWIO', 'NDHWC'), feature_group_count=groups, preferred_element_type=jnp.float32)

def pad_depth(volume):
    return jnp.pad(volume, ((0, 0), (1, 1), (0, 0), (0, 0), (0, 0)))

def flip_kernel(kernel, groups):
    group_width = kernel.shape[3]
    split_kernel = kernel.reshape(3, 3, 3, group_width, groups, group_width)
    turned = jnp.transpose(split_kernel, (0, 1, 2, 5, 4, 3))[::-1, ::-1, ::-1]
    return turned.reshape(3, 3, 3, group_width, groups * group_width)

def kernel_grad(padded, slopes, group_width):
    full = jnp.pad(padded, ((0, 0), (0, 0), (1, 1), (1, 1), (0, 0)))
    depth, height, width, channels = (slopes.shape[1], slopes.shape[2], slopes.shape[3], slopes.shape[4])
    groups = channels // group_width
    right = slopes.reshape(-1, groups, group_width).astype(jnp.float32)
    terms = []
    for first in range(3):
        for second in range(3):
            for third in range(3):
                piece = full[:, first:first + depth, second:second + height, third:third + width, :]
                left = piece.reshape(-1, groups, group_width).astype(jnp.float32)
                block = jnp.einsum('ngi,ngo->igo', left, right)
                terms.append(block.reshape(group_width, channels))
    return jnp.stack(terms).reshape(3, 3, 3, group_width, channels)

def sample_terms(volume, grad_volume, w_in, w_out, w_group):
    channels = volume.shape[-1]
    group_width = w_group.shape[3]
    groups = channels // group_width
    shape = (1,) + volume.shape
    rows_in = volume.reshape(-1, channels)
    rows_grad = grad_volume.reshape(-1, channels)
    pre_first = jnp.dot(rows_in, w_in, preferred_element_type=jnp.float32)
    first_act = jax.nn.silu(pre_first).astype(jnp.bfloat16).reshape(shape)
    back_second = jnp.dot(rows_grad, w_out.T, preferred_element_type=jnp.float32).astype(jnp.bfloat16).reshape(shape)
    padded = pad_depth(first_act)
    pre_second = group_conv(padded, w_group, groups)
    second_act = jax.nn.silu(pre_second).astype(jnp.bfloat16)
    slopes = (back_second.astype(jnp.float32) * silu_slope(pre_second)).astype(jnp.bfloat16)
    kernel_part = kernel_grad(padded, slopes, group_width)
    back_first = group_conv(pad_depth(slopes), flip_kernel(w_group, groups), groups).astype(jnp.bfloat16)
    grad_out_part = jnp.dot(second_act.reshape(-1, channels).T, rows_grad, preferred_element_type=jnp.float32)
    slope_first = (back_first.reshape(-1, channels).astype(jnp.float32) * silu_slope(pre_first)).astype(jnp.bfloat16)
    grad_in_part = jnp.dot(rows_in.T, slope_first, preferred_element_type=jnp.float32)
    back_input = rows_grad.astype(jnp.float32) + jnp.dot(slope_first, w_in.T, preferred_element_type=jnp.float32)
    return (back_input.astype(jnp.bfloat16).reshape(volume.shape), grad_in_part, grad_out_part, kernel_part)

def reference(inputs, cotangent, w_in, w_out, w_group):
    backs, grads_in, grads_out, grads_group = ([], [], [], [])
    for section in range(N_PIPE):

        def one_sample(pair):
            return sample_terms(pair[0], pair[1], w_in[section], w_out[section], w_group[section])
        back, part_in, part_out, part_group = lax.map(one_sample, (inputs[section], cotangent[section]))
        backs.append(back)
        grads_in.append(lax.optimization_barrier(jnp.sum(part_in, axis=0)))
        grads_out.append(lax.optimization_barrier(jnp.sum(part_out, axis=0)))
        grads_group.append(lax.optimization_barrier(jnp.sum(part_group, axis=0)))
    backs.append(jnp.zeros_like(backs[0]))
    section_grad = jnp.stack(backs[1:])
    return (section_grad, jnp.stack(grads_in), jnp.stack(grads_out), jnp.stack(grads_group))
```

```python
import functools

import jax
import jax.numpy as jnp
from jax import lax
from jax.experimental import pallas as pl
from jax.experimental.pallas import tpu as pltpu
from jax.sharding import PartitionSpec as P

F32 = jnp.float32
BF16 = jnp.bfloat16

C = 256
GW = 8
SIDE = 16
CELLS = SIDE * SIDE
TAPS = 27
PAD_ROWS = CELLS + 2 * SIDE
NDEV = 128
INTERPRET = False

NT = (((1,), (1,)), ((), ()))


def dot(a, b):
    return jnp.dot(a, b, preferred_element_type=F32)


def dot_nt(a, b):
    return lax.dot_general(a, b, NT, preferred_element_type=F32)


def sigmoid(v):
    return 1.0 / (1.0 + jnp.exp(-v))


def column():
    return lax.broadcasted_iota(jnp.int32, (CELLS, C), 0) % SIDE


def fill(buf, plane, sign):
    zeros = jnp.zeros((SIDE, 3 * C), BF16)
    buf[0:SIDE, :] = zeros
    buf[SIDE + CELLS :, :] = zeros
    col = column()
    ahead = jnp.where(col < SIDE - 1, pltpu.roll(plane, CELLS - 1, 0), 0.0)
    behind = jnp.where(col > 0, pltpu.roll(plane, 1, 0), 0.0)
    left, right = (behind, ahead) if sign > 0 else (ahead, behind)
    buf[SIDE : SIDE + CELLS, 0:C] = left.astype(BF16)
    buf[SIDE : SIDE + CELLS, C : 2 * C] = plane.astype(BF16)
    buf[SIDE : SIDE + CELLS, 2 * C :] = right.astype(BF16)


def conv_plane(buf, wd, depth):
    total = None
    for row in range(3):
        start = (depth * 3 + row) * 3 * C
        term = dot(buf[row * SIDE : row * SIDE + CELLS, :], wd[start : start + 3 * C, :])
        total = term if total is None else total + term
    return total


def conv_plane_back(buf, wd, depth):
    total = None
    for row in range(3):
        for col in range(3):
            start = ((depth * 3 + row) * 3 + col) * C
            rows = (2 - row) * SIDE
            term = dot_nt(
                buf[rows : rows + CELLS, col * C : (col + 1) * C], wd[start : start + C, :]
            )
            total = term if total is None else total + term
    return total


def own_kernel(x, cot, w_in, w_out, wg, slope1, h1, dh2, wd, xt, z2p, buf):
    z1 = dot(x[...], w_in[...])
    sig = sigmoid(z1)
    slope1[...] = sig * (1.0 + z1 * (1.0 - sig))
    act = (z1 * sig).astype(BF16)
    h1[...] = act
    dh2[...] = dot_nt(cot[...], w_out[...]).astype(BF16)
    same = (
        lax.broadcasted_iota(jnp.int32, (C, C), 0) // GW
        == lax.broadcasted_iota(jnp.int32, (C, C), 1) // GW
    )
    taps = wg[...].astype(F32)
    for k in range(TAPS):
        rows = jnp.broadcast_to(taps[k * GW : (k + 1) * GW, :][None], (C // GW, GW, C))
        wd[k * C : (k + 1) * C, :] = jnp.where(same, rows.reshape(C, C), 0.0).astype(BF16)
    fill(buf, act.astype(F32), 1)
    z2p[...] = conv_plane(buf, wd, 1)
    xt[...] = x[...].T


def middle_kernel(xl, xr, w_in, wd, z2p, dh2, h1l, h1r, h2, dz2, bufl, bufr):
    total = z2p[...]
    for x, h1, buf, depth in ((xl, h1l, bufl, 0), (xr, h1r, bufr, 2)):
        z1 = dot(x[...], w_in[...])
        act = (z1 * sigmoid(z1)).astype(BF16)
        h1[...] = act
        fill(buf, act.astype(F32), 1)
        total = total + conv_plane(buf, wd, depth)
    sig = sigmoid(total)
    h2[...] = (total * sig).astype(BF16)
    slope = sig * (1.0 + total * (1.0 - sig))
    dz2[...] = (dh2[...].astype(F32) * slope).astype(BF16)


def grads_kernel(h1l, h1, h1r, h2, cot, dz2, wd, grad_out, gg, dh1p, buf, ht, taps):
    fill(buf, dz2[...].astype(F32), -1)
    dh1p[...] = conv_plane_back(buf, wd, 1)
    half = C // 2
    outer = dot(h2[...].T, cot[...])
    for side in range(2):
        grad_out[side] = outer[:, side * half : (side + 1) * half]
    for depth, plane in enumerate((h1l, h1, h1r)):
        turned = plane[...].T
        for side in range(2):
            ht[side, depth * half : (depth + 1) * half, :] = turned[
                side * half : (side + 1) * half, :
            ]
    groups = half // GW
    same = (
        lax.broadcasted_iota(jnp.int32, (half, half), 0) // GW
        == lax.broadcasted_iota(jnp.int32, (half, half), 1) // GW
    )
    taps[...] = jnp.zeros_like(taps)
    for row in range(3):
        for col in range(3):
            rows = (2 - row) * SIDE
            for side in range(2):
                lanes = col * C + side * half
                full = dot(ht[side], buf[rows : rows + CELLS, lanes : lanes + half])
                for depth in range(3):
                    block = jnp.where(same, full[depth * half : (depth + 1) * half, :], 0.0)
                    k = (depth * 3 + row) * 3 + col
                    taps[k * GW : (k + 1) * GW, side * half : (side + 1) * half] = jnp.sum(
                        block.reshape(groups, GW, half), axis=0
                    )
    gg[...] = taps[...].T.reshape(C // GW, GW, C).astype(BF16)


def final_kernel(dz2l, dz2r, dh1p, wd, slope1, xt, grad_out, gg, dz1, pay, bufl, bufr, grad, pack):
    fill(bufl, dz2l[...].astype(F32), -1)
    fill(bufr, dz2r[...].astype(F32), -1)
    total = dh1p[...] + conv_plane_back(bufl, wd, 2) + conv_plane_back(bufr, wd, 0)
    back = (total.astype(BF16).astype(F32) * slope1[...]).astype(BF16)
    dz1[...] = back
    half = C // 2
    outer = dot(xt[...], back)
    for side in range(2):
        grad[side] = outer[:, side * half : (side + 1) * half]
    for which, source in enumerate((grad, grad_out)):
        for parity in range(2):
            for side in range(2):
                pack[pl.ds(which * 4 + parity * 2 + side, NDEV, stride=8), :] = source.at[
                    side
                ][pl.ds(parity, NDEV, stride=2), :]
    pay[:, :, 0:half] = pack[...].reshape(NDEV, 8, half).astype(BF16)
    blocks = C // GW
    for start in range(0, NDEV, blocks):
        pay[start : start + blocks, :, half:] = gg[...]


def dx_kernel(cot, dz1, w_in, dx):
    dx[...] = (cot[...].astype(F32) + dot_nt(dz1[...], w_in[...])).astype(BF16)


def sum_kernel(got, grad_in, grad_out, gg):
    total = jnp.sum(got[...].astype(F32), axis=0)
    half = C // 2
    for which, out in enumerate((grad_in, grad_out)):
        for parity in range(2):
            for side in range(2):
                row = which * 4 + parity * 2 + side
                out[parity : parity + 1, side * half : (side + 1) * half] = total[
                    row : row + 1, 0:half
                ]
    gg[...] = total[:, half:].T[0 : TAPS * GW, :]


def call(kernel, outs, scratch, flops, *args):
    shapes = [jax.ShapeDtypeStruct(shape, dtype) for shape, dtype in outs]
    size = sum(a.size * a.dtype.itemsize for a in (*args, *shapes))
    return pl.pallas_call(
        kernel,
        out_shape=shapes,
        in_specs=[pl.BlockSpec(memory_space=pltpu.VMEM)] * len(args),
        out_specs=[pl.BlockSpec(memory_space=pltpu.VMEM)] * len(outs),
        scratch_shapes=[pltpu.VMEM(shape, dtype) for shape, dtype in scratch],
        cost_estimate=pl.CostEstimate(flops=flops, bytes_accessed=size, transcendentals=0),
        compiler_params=pltpu.CompilerParams(vmem_limit_bytes=40 * 1024 * 1024),
        interpret=INTERPRET,
    )(*args)


PLANE = (CELLS, C)
BUF = ((PAD_ROWS, 3 * C), BF16)
TILE = 2 * C**3


def own_stage(x, cot, w_in, w_out, wg):
    return call(
        own_kernel,
        [(PLANE, F32), (PLANE, BF16), (PLANE, BF16), ((TAPS * C, C), BF16), (PLANE, BF16), (PLANE, F32)],
        [BUF],
        11 * TILE,
        x, cot, w_in, w_out, wg,
    )


def middle_stage(*args):
    return call(middle_kernel, [(PLANE, BF16)] * 4, [BUF, BUF], 20 * TILE, *args)


def grads_stage(*args):
    return call(
        grads_kernel,
        [((2, C, C // 2), F32), ((C // GW, GW, C), BF16), (PLANE, F32)],
        [BUF, ((2, 3 * C // 2, CELLS), BF16), ((C, C), F32)],
        37 * TILE,
        *args,
    )


def final_stage(*args):
    return call(
        final_kernel,
        [(PLANE, BF16), ((NDEV, 8, 3 * C // 2), BF16)],
        [BUF, BUF, ((2, C, C // 2), F32), ((NDEV * 8, C // 2), F32)],
        19 * TILE,
        *args,
    )


def dx_stage(*args):
    return call(dx_kernel, [(PLANE, BF16)], [], TILE, *args)[0]


def sum_stage(got):
    return call(sum_kernel, [((2, C), F32), ((2, C), F32), ((TAPS * GW, GW), F32)], [], 1000, got)


def shifted(value, axis, steps):
    count = lax.axis_size(axis)
    first, last = (max(0, -steps), min(count, count - steps))
    return lax.ppermute(value, axis, [(source, source + steps) for source in range(first, last)])


def per_device(inputs, cotangent, w_in, w_out, w_group):
    shape = inputs.shape
    x = inputs.reshape(PLANE)
    cot = cotangent.reshape(PLANE)
    w_in = w_in.reshape(C, C)
    w_out = w_out.reshape(C, C)
    wg = w_group.reshape(TAPS * GW, C)
    xl = shifted(x, "sg", 1)
    xr = shifted(x, "sg", -1)
    slope1, h1, dh2, wd, xt, z2p = own_stage(x, cot, w_in, w_out, wg)
    h1l, h1r, h2, dz2 = middle_stage(xl, xr, w_in, wd, z2p, dh2)
    dz2l = shifted(dz2, "sg", 1)
    dz2r = shifted(dz2, "sg", -1)
    grad_out, gg, dh1p = grads_stage(h1l, h1, h1r, h2, cot, dz2, wd)
    dz1, pay = final_stage(dz2l, dz2r, dh1p, wd, slope1, xt, grad_out, gg)
    got = lax.all_to_all(pay, ("dp", "sg"), 0, 0, tiled=True)
    dx = dx_stage(cot, dz1, w_in)
    section_grad = shifted(dx.reshape(shape), "pipe", -1)
    grad_in, grad_out, gg = sum_stage(got)
    return (
        section_grad,
        grad_in[None],
        grad_out[None],
        gg.reshape(1, 3, 3, 3, GW, GW),
    )


def solution(mesh):
    placed = (
        P("pipe", "dp", "sg", None, None, None),
        P("pipe", "dp", "sg", None, None, None),
        P("pipe", None, None),
        P("pipe", None, None),
        P("pipe", None, None, None, None, None),
    )
    return jax.shard_map(
        per_device,
        mesh=mesh,
        in_specs=placed,
        out_specs=(
            P("pipe", "dp", "sg", None, None, None),
            P("pipe", ("dp", "sg"), None),
            P("pipe", ("dp", "sg"), None),
            P("pipe", None, None, None, None, "sg"),
        ),
        check_vma=False,
    )
```

```python
import functools

import jax
import jax.numpy as jnp
from jax import lax
from jax.experimental import pallas as pl
from jax.experimental.pallas import tpu as pltpu
from jax.sharding import PartitionSpec as P

F32 = jnp.float32
BF16 = jnp.bfloat16

C = 256
GW = 8
SIDE = 16
CELLS = SIDE * SIDE
TAPS = 27
PAD_ROWS = CELLS + 2 * SIDE
NDEV = 128
INTERPRET = False

NT = (((1,), (1,)), ((), ()))


def dot(a, b):
    return jnp.dot(a, b, preferred_element_type=F32)


def dot_nt(a, b):
    return lax.dot_general(a, b, NT, preferred_element_type=F32)


def sigmoid(v):
    return 1.0 / (1.0 + jnp.exp(-v))


def column():
    return lax.broadcasted_iota(jnp.int32, (CELLS, C), 0) % SIDE


def fill(buf, plane, sign):
    zeros = jnp.zeros((SIDE, 3 * C), BF16)
    buf[0:SIDE, :] = zeros
    buf[SIDE + CELLS :, :] = zeros
    col = column()
    ahead = jnp.where(col < SIDE - 1, pltpu.roll(plane, CELLS - 1, 0), 0.0)
    behind = jnp.where(col > 0, pltpu.roll(plane, 1, 0), 0.0)
    left, right = (behind, ahead) if sign > 0 else (ahead, behind)
    buf[SIDE : SIDE + CELLS, 0:C] = left.astype(BF16)
    buf[SIDE : SIDE + CELLS, C : 2 * C] = plane.astype(BF16)
    buf[SIDE : SIDE + CELLS, 2 * C :] = right.astype(BF16)


def conv_plane(buf, wd, depth):
    total = None
    for row in range(3):
        start = (depth * 3 + row) * 3 * C
        term = dot(buf[row * SIDE : row * SIDE + CELLS, :], wd[start : start + 3 * C, :])
        total = term if total is None else total + term
    return total


def conv_plane_back(buf, wd, depth):
    total = None
    for row in range(3):
        for col in range(3):
            start = ((depth * 3 + row) * 3 + col) * C
            rows = (2 - row) * SIDE
            term = dot_nt(
                buf[rows : rows + CELLS, col * C : (col + 1) * C], wd[start : start + C, :]
            )
            total = term if total is None else total + term
    return total


def spread(wg, wd, which):
    same = (
        lax.broadcasted_iota(jnp.int32, (C, C), 0) // GW
        == lax.broadcasted_iota(jnp.int32, (C, C), 1) // GW
    )
    taps = wg[...].astype(F32)
    for k in which:
        rows = jnp.broadcast_to(taps[k * GW : (k + 1) * GW, :][None], (C // GW, GW, C))
        wd[k * C : (k + 1) * C, :] = jnp.where(same, rows.reshape(C, C), 0.0).astype(BF16)


def own_kernel(
    x_hbm, cot_hbm, w_in_hbm, w_out_hbm, wg_hbm,
    slope1, h1, dh2, wd, z2p, x, cot, w_in,
    buf, w_out, wg, sems,
):
    copies = [
        pltpu.make_async_copy(source, target, sems.at[i])
        for i, (source, target) in enumerate(
            ((wg_hbm, wg), (x_hbm, x), (w_in_hbm, w_in), (cot_hbm, cot), (w_out_hbm, w_out))
        )
    ]
    for copy in copies:
        copy.start()
    copies[0].wait()
    spread(wg, wd, range(TAPS))
    for copy in copies[1:]:
        copy.wait()
    z1 = dot(x[...], w_in[...])
    sig = sigmoid(z1)
    slope1[...] = sig * (1.0 + z1 * (1.0 - sig))
    act = (z1 * sig).astype(BF16)
    h1[...] = act
    dh2[...] = dot_nt(cot[...], w_out[...]).astype(BF16)
    fill(buf, act.astype(F32), 1)
    z2p[...] = conv_plane(buf, wd, 1)


def middle_kernel(
    xl, x, xr, cot, w_in, wd, z2p, dh2, h1, slope1,
    own, left, right, pay,
    bufl, bufr, buf, ht, slopes, taps, grads, pack,
):
    half = C // 2
    total = z2p[...]
    for x_next, b, depth in ((xl, bufl, 0), (xr, bufr, 2)):
        z1 = dot(x_next[...], w_in[...])
        sig = sigmoid(z1)
        slopes[depth // 2] = sig * (1.0 + z1 * (1.0 - sig))
        fill(b, (z1 * sig).astype(BF16).astype(F32), 1)
        total = total + conv_plane(b, wd, depth)
    sig = sigmoid(total)
    h2 = (total * sig).astype(BF16)
    slope = sig * (1.0 + total * (1.0 - sig))
    back = (dh2[...].astype(F32) * slope).astype(BF16)
    fill(buf, back.astype(F32), -1)
    outer = dot(h2.T, cot[...])
    for side in range(2):
        grads[2 + side] = outer[:, side * half : (side + 1) * half]
    share = (conv_plane_back(buf, wd, 1) * slope1[...]).astype(BF16)
    own[...] = share
    outer = dot(x[...].T, share)
    for x_next, out, depth in ((xl, left, 0), (xr, right, 2)):
        share = (conv_plane_back(buf, wd, depth) * slopes[depth // 2]).astype(BF16)
        outer = outer + dot(x_next[...].T, share)
        out[...] = share
    for side in range(2):
        grads[side] = outer[:, side * half : (side + 1) * half]
    for depth, plane in enumerate((bufl, None, bufr)):
        value = h1[...] if plane is None else plane[SIDE : SIDE + CELLS, C : 2 * C]
        turned = value.T
        for side in range(2):
            ht[side, depth * half : (depth + 1) * half, :] = turned[
                side * half : (side + 1) * half, :
            ]
    groups = half // GW
    same = (
        lax.broadcasted_iota(jnp.int32, (half, half), 0) // GW
        == lax.broadcasted_iota(jnp.int32, (half, half), 1) // GW
    )
    taps[TAPS * GW :, :] = jnp.zeros((C - TAPS * GW, C), F32)
    for row in range(3):
        for col in range(3):
            rows = (2 - row) * SIDE
            for side in range(2):
                lanes = col * C + side * half
                full = dot(ht[side], buf[rows : rows + CELLS, lanes : lanes + half])
                for depth in range(3):
                    block = jnp.where(same, full[depth * half : (depth + 1) * half, :], 0.0)
                    k = (depth * 3 + row) * 3 + col
                    taps[k * GW : (k + 1) * GW, side * half : (side + 1) * half] = jnp.sum(
                        block.reshape(groups, GW, half), axis=0
                    )
    for which in range(2):
        for parity in range(2):
            for side in range(2):
                pack[pl.ds(which * 4 + parity * 2 + side, NDEV, stride=8), :] = grads.at[
                    which * 2 + side
                ][pl.ds(parity, NDEV, stride=2), :]
    blocks = C // GW
    packed = pack[...].reshape(NDEV, 8, half).astype(BF16)
    gg = taps[...].T.reshape(blocks, GW, C).astype(BF16)
    for part in range(NDEV // blocks):
        pay[:, :, part * half : (part + 1) * half] = packed[part * blocks : (part + 1) * blocks]
    pay[:, :, 4 * half :] = gg


def dx_kernel(own, left, right, cot, w_in, dx, dxl, dxr):
    dx[...] = (cot[...].astype(F32) + dot_nt(own[...], w_in[...])).astype(BF16)
    dxl[...] = dot_nt(left[...], w_in[...]).astype(BF16)
    dxr[...] = dot_nt(right[...], w_in[...]).astype(BF16)


def first_sum_kernel(got, pay):
    total = jnp.sum(got[...].astype(F32), axis=0)
    half = C // 2
    for part in range(4):
        pay[part, :, 0:half] = total[:, part * half : (part + 1) * half]
        pay[part, :, half:] = total[:, 4 * half :]


def sum_kernel(got, dx, dxl, dxr, grad_in, grad_out, gg, section):
    section[...] = (
        dx[...].astype(F32) + (dxl[...].astype(F32) + dxr[...].astype(F32))
    ).astype(BF16)
    total = jnp.sum(got[...].astype(F32), axis=0)
    half = C // 2
    for which, out in enumerate((grad_in, grad_out)):
        for parity in range(2):
            for side in range(2):
                row = which * 4 + parity * 2 + side
                out[parity : parity + 1, side * half : (side + 1) * half] = total[
                    row : row + 1, 0:half
                ]
    gg[...] = total[:, half:].T[0 : TAPS * GW, :]


def call(kernel, outs, scratch, flops, *args, space=pltpu.VMEM):
    shapes = [jax.ShapeDtypeStruct(shape, dtype) for shape, dtype in outs]
    size = sum(a.size * a.dtype.itemsize for a in (*args, *shapes))
    return pl.pallas_call(
        kernel,
        out_shape=shapes,
        in_specs=[pl.BlockSpec(memory_space=space)] * len(args),
        out_specs=[pl.BlockSpec(memory_space=pltpu.VMEM)] * len(outs),
        scratch_shapes=[
            pltpu.VMEM(*entry) if isinstance(entry, tuple) else entry for entry in scratch
        ],
        cost_estimate=pl.CostEstimate(flops=flops, bytes_accessed=size, transcendentals=0),
        compiler_params=pltpu.CompilerParams(vmem_limit_bytes=8 * 1024 * 1024),
        interpret=INTERPRET,
    )(*args)


PLANE = (CELLS, C)
BUF = ((PAD_ROWS, 3 * C), BF16)
PAY = (C // GW, 8, 3 * C)
TILE = 2 * C**3


def own_stage(x, cot, w_in, w_out, wg):
    return call(
        own_kernel,
        [(PLANE, F32), (PLANE, BF16), (PLANE, BF16), ((TAPS * C, C), BF16), (PLANE, F32)]
        + [(PLANE, BF16)] * 3,
        [BUF, (PLANE, BF16), ((TAPS * GW, C), BF16), pltpu.SemaphoreType.DMA((5,))],
        11 * TILE,
        x, cot, w_in, w_out, wg,
        space=pltpu.HBM,
    )


def middle_stage(*args):
    return call(
        middle_kernel,
        [(PLANE, BF16)] * 3 + [(PAY, BF16)],
        [
            BUF, BUF, BUF,
            ((2, 3 * C // 2, CELLS), BF16),
            ((2, CELLS, C), F32),
            ((C, C), F32),
            ((4, C, C // 2), F32),
            ((NDEV * 8, C // 2), F32),
        ],
        80 * TILE,
        *args,
    )


def dx_stage(*args):
    return call(dx_kernel, [(PLANE, BF16)] * 3, [], 3 * TILE, *args)


def first_sum_stage(got):
    return call(first_sum_kernel, [((4, 8, 3 * C // 2), F32)], [], 1000, got)[0]


def sum_stage(*args):
    return call(
        sum_kernel,
        [((2, C), F32), ((2, C), F32), ((TAPS * GW, GW), F32), (PLANE, BF16)],
        [],
        1000,
        *args,
    )


def shifted(value, steps):
    pipes, planes = lax.axis_size("pipe"), lax.axis_size("sg")
    pairs = [
        (pipe * planes + plane, (pipe + steps[0]) * planes + plane + steps[1])
        for pipe in range(pipes)
        for plane in range(planes)
        if 0 <= pipe + steps[0] < pipes and 0 <= plane + steps[1] < planes
    ]
    return lax.ppermute(value, ("pipe", "sg"), pairs)


def per_device(inputs, cotangent, w_in, w_out, w_group):
    shape = inputs.shape
    x = inputs.reshape(PLANE)
    cot = cotangent.reshape(PLANE)
    w_in = w_in.reshape(C, C)
    w_out = w_out.reshape(C, C)
    wg = w_group.reshape(TAPS * GW, C)
    xl = shifted(x, (0, 1))
    xr = shifted(x, (0, -1))
    kept = [
        pltpu.with_memory_space_constraint(value, pltpu.HBM)
        for value in (x, cot, w_in, w_out, wg)
    ]
    slope1, h1, dh2, wd, z2p, x, cot, w_in = own_stage(*kept)
    own, left, right, pay = middle_stage(xl, x, xr, cot, w_in, wd, z2p, dh2, h1, slope1)
    dx, dxl, dxr = dx_stage(own, left, right, cot, w_in)
    part = first_sum_stage(lax.all_to_all(pay, "sg", 0, 0, tiled=True))
    got = lax.all_to_all(part, "dp", 0, 0, tiled=True)
    grad_in, grad_out, gg, section_grad = sum_stage(
        got, shifted(dx, (-1, 0)), shifted(dxl, (-1, -1)), shifted(dxr, (-1, 1))
    )
    return (
        section_grad.reshape(shape),
        grad_in[None],
        grad_out[None],
        gg.reshape(1, 3, 3, 3, GW, GW),
    )


def solution(mesh):
    placed = (
        P("pipe", "dp", "sg", None, None, None),
        P("pipe", "dp", "sg", None, None, None),
        P("pipe", None, None),
        P("pipe", None, None),
        P("pipe", None, None, None, None, None),
    )
    return jax.shard_map(
        per_device,
        mesh=mesh,
        in_specs=placed,
        out_specs=(
            P("pipe", "dp", "sg", None, None, None),
            P("pipe", ("dp", "sg"), None),
            P("pipe", ("dp", "sg"), None),
            P("pipe", None, None, None, None, "sg"),
        ),
        check_vma=False,
    )
```

```python
import functools

import jax
import jax.numpy as jnp
from jax import lax
from jax.experimental import pallas as pl
from jax.experimental.pallas import tpu as pltpu
from jax.sharding import PartitionSpec as P

F32 = jnp.float32
BF16 = jnp.bfloat16

C = 256
GW = 8
SIDE = 16
CELLS = SIDE * SIDE
TAPS = 27
PAD_ROWS = CELLS + 2 * SIDE
NDEV = 128
INTERPRET = False

NT = (((1,), (1,)), ((), ()))


def dot(a, b):
    return jnp.dot(a, b, preferred_element_type=F32)


def dot_nt(a, b):
    return lax.dot_general(a, b, NT, preferred_element_type=F32)


def sigmoid(v):
    return 1.0 / (1.0 + jnp.exp(-v))


def column():
    return lax.broadcasted_iota(jnp.int32, (CELLS, C), 0) % SIDE


def fill(buf, plane, sign):
    zeros = jnp.zeros((SIDE, 3 * C), BF16)
    buf[0:SIDE, :] = zeros
    buf[SIDE + CELLS :, :] = zeros
    col = column()
    ahead = jnp.where(col < SIDE - 1, pltpu.roll(plane, CELLS - 1, 0), 0.0)
    behind = jnp.where(col > 0, pltpu.roll(plane, 1, 0), 0.0)
    left, right = (behind, ahead) if sign > 0 else (ahead, behind)
    buf[SIDE : SIDE + CELLS, 0:C] = left.astype(BF16)
    buf[SIDE : SIDE + CELLS, C : 2 * C] = plane.astype(BF16)
    buf[SIDE : SIDE + CELLS, 2 * C :] = right.astype(BF16)


def conv_plane(buf, wd, depth):
    total = None
    for row in range(3):
        start = (depth * 3 + row) * 3 * C
        term = dot(buf[row * SIDE : row * SIDE + CELLS, :], wd[start : start + 3 * C, :])
        total = term if total is None else total + term
    return total


def conv_plane_back(buf, wd, depth):
    total = None
    for row in range(3):
        for col in range(3):
            start = ((depth * 3 + row) * 3 + col) * C
            rows = (2 - row) * SIDE
            term = dot_nt(
                buf[rows : rows + CELLS, col * C : (col + 1) * C], wd[start : start + C, :]
            )
            total = term if total is None else total + term
    return total


def spread(wg, wd, which):
    same = (
        lax.broadcasted_iota(jnp.int32, (C, C), 0) // GW
        == lax.broadcasted_iota(jnp.int32, (C, C), 1) // GW
    )
    taps = wg[...].astype(F32)
    for k in which:
        rows = jnp.broadcast_to(taps[k * GW : (k + 1) * GW, :][None], (C // GW, GW, C))
        wd[k * C : (k + 1) * C, :] = jnp.where(same, rows.reshape(C, C), 0.0).astype(BF16)


def own_kernel(
    x_hbm, cot_hbm, w_in_hbm, w_out_hbm, wg_hbm,
    slope1, h1, dh2, wd, z2p, x, cot, w_in,
    buf, w_out, wg, sems,
):
    copies = [
        pltpu.make_async_copy(source, target, sems.at[i])
        for i, (source, target) in enumerate(
            ((wg_hbm, wg), (x_hbm, x), (w_in_hbm, w_in), (cot_hbm, cot), (w_out_hbm, w_out))
        )
    ]
    for copy in copies:
        copy.start()
    copies[0].wait()
    spread(wg, wd, range(TAPS))
    for copy in copies[1:]:
        copy.wait()
    z1 = dot(x[...], w_in[...])
    sig = sigmoid(z1)
    slope1[...] = sig * (1.0 + z1 * (1.0 - sig))
    act = (z1 * sig).astype(BF16)
    h1[...] = act
    dh2[...] = dot_nt(cot[...], w_out[...]).astype(BF16)
    fill(buf, act.astype(F32), 1)
    z2p[...] = conv_plane(buf, wd, 1)


def middle_kernel(
    near, far, x, cot, w_in, wd, z2p, dh2, h1, slope1,
    own, to_near, to_far, pay,
    bufl, bufr, buf, ht, slopes, taps, grads, pack, xl, xr, left, right,
):
    half = C // 2
    even = lax.axis_index("sg") % 2 == 0

    def swap(pair, out):
        @pl.when(even)
        def _():
            out[0][...] = pair[1][...]
            out[1][...] = pair[0][...]

        @pl.when(jnp.logical_not(even))
        def _():
            out[0][...] = pair[0][...]
            out[1][...] = pair[1][...]

    swap((near, far), (xl, xr))
    total = z2p[...]
    for x_next, b, depth in ((xl, bufl, 0), (xr, bufr, 2)):
        z1 = dot(x_next[...], w_in[...])
        sig = sigmoid(z1)
        slopes[depth // 2] = sig * (1.0 + z1 * (1.0 - sig))
        fill(b, (z1 * sig).astype(BF16).astype(F32), 1)
        total = total + conv_plane(b, wd, depth)
    sig = sigmoid(total)
    h2 = (total * sig).astype(BF16)
    slope = sig * (1.0 + total * (1.0 - sig))
    back = (dh2[...].astype(F32) * slope).astype(BF16)
    fill(buf, back.astype(F32), -1)
    outer = dot(h2.T, cot[...])
    for side in range(2):
        grads[2 + side] = outer[:, side * half : (side + 1) * half]
    share = (conv_plane_back(buf, wd, 1) * slope1[...]).astype(BF16)
    own[...] = share
    outer = dot(x[...].T, share)
    for x_next, out, depth in ((xl, left, 0), (xr, right, 2)):
        share = (conv_plane_back(buf, wd, depth) * slopes[depth // 2]).astype(BF16)
        outer = outer + dot(x_next[...].T, share)
        out[...] = share
    swap((left, right), (to_near, to_far))
    for side in range(2):
        grads[side] = outer[:, side * half : (side + 1) * half]
    for depth, plane in enumerate((bufl, None, bufr)):
        value = h1[...] if plane is None else plane[SIDE : SIDE + CELLS, C : 2 * C]
        turned = value.T
        for side in range(2):
            ht[side, depth * half : (depth + 1) * half, :] = turned[
                side * half : (side + 1) * half, :
            ]
    groups = half // GW
    same = (
        lax.broadcasted_iota(jnp.int32, (half, half), 0) // GW
        == lax.broadcasted_iota(jnp.int32, (half, half), 1) // GW
    )
    taps[TAPS * GW :, :] = jnp.zeros((C - TAPS * GW, C), F32)
    for row in range(3):
        for col in range(3):
            rows = (2 - row) * SIDE
            for side in range(2):
                lanes = col * C + side * half
                full = dot(ht[side], buf[rows : rows + CELLS, lanes : lanes + half])
                for depth in range(3):
                    block = jnp.where(same, full[depth * half : (depth + 1) * half, :], 0.0)
                    k = (depth * 3 + row) * 3 + col
                    taps[k * GW : (k + 1) * GW, side * half : (side + 1) * half] = jnp.sum(
                        block.reshape(groups, GW, half), axis=0
                    )
    for which in range(2):
        for parity in range(2):
            for side in range(2):
                pack[pl.ds(which * 4 + parity * 2 + side, NDEV, stride=8), :] = grads.at[
                    which * 2 + side
                ][pl.ds(parity, NDEV, stride=2), :]
    blocks = C // GW
    packed = pack[...].reshape(NDEV, 8, half).astype(BF16)
    gg = taps[...].T.reshape(blocks, GW, C).astype(BF16)
    for part in range(NDEV // blocks):
        pay[:, :, part * half : (part + 1) * half] = packed[part * blocks : (part + 1) * blocks]
    pay[:, :, 4 * half :] = gg


def own_dx_kernel(own, cot, w_in, dx):
    dx[...] = (cot[...].astype(F32) + dot_nt(own[...], w_in[...])).astype(BF16)


def pair_dx_kernel(near, far, w_in, dx_near, dx_far):
    dx_near[...] = dot_nt(near[...], w_in[...]).astype(BF16)
    dx_far[...] = dot_nt(far[...], w_in[...]).astype(BF16)


def first_sum_kernel(got, pay):
    total = jnp.sum(got[...].astype(F32), axis=0)
    half = C // 2
    for part in range(4):
        pay[part, :, 0:half] = total[:, part * half : (part + 1) * half]
        pay[part, :, half:] = total[:, 4 * half :]


def sum_kernel(got, dx, dxl, dxr, grad_in, grad_out, gg, section):
    section[...] = (
        dx[...].astype(F32) + (dxl[...].astype(F32) + dxr[...].astype(F32))
    ).astype(BF16)
    total = jnp.sum(got[...].astype(F32), axis=0)
    half = C // 2
    for which, out in enumerate((grad_in, grad_out)):
        for parity in range(2):
            for side in range(2):
                row = which * 4 + parity * 2 + side
                out[parity : parity + 1, side * half : (side + 1) * half] = total[
                    row : row + 1, 0:half
                ]
    gg[...] = total[:, half:].T[0 : TAPS * GW, :]


def call(kernel, outs, scratch, flops, *args, space=pltpu.VMEM):
    shapes = [jax.ShapeDtypeStruct(shape, dtype) for shape, dtype in outs]
    size = sum(a.size * a.dtype.itemsize for a in (*args, *shapes))
    return pl.pallas_call(
        kernel,
        out_shape=shapes,
        in_specs=[pl.BlockSpec(memory_space=space)] * len(args),
        out_specs=[pl.BlockSpec(memory_space=pltpu.VMEM)] * len(outs),
        scratch_shapes=[
            pltpu.VMEM(*entry) if isinstance(entry, tuple) else entry for entry in scratch
        ],
        cost_estimate=pl.CostEstimate(flops=flops, bytes_accessed=size, transcendentals=0),
        compiler_params=pltpu.CompilerParams(vmem_limit_bytes=8 * 1024 * 1024),
        interpret=INTERPRET,
    )(*args)


PLANE = (CELLS, C)
BUF = ((PAD_ROWS, 3 * C), BF16)
PAY = (C // GW, 8, 3 * C)
TILE = 2 * C**3


def own_stage(x, cot, w_in, w_out, wg):
    return call(
        own_kernel,
        [(PLANE, F32), (PLANE, BF16), (PLANE, BF16), ((TAPS * C, C), BF16), (PLANE, F32)]
        + [(PLANE, BF16)] * 3,
        [BUF, (PLANE, BF16), ((TAPS * GW, C), BF16), pltpu.SemaphoreType.DMA((5,))],
        11 * TILE,
        x, cot, w_in, w_out, wg,
        space=pltpu.HBM,
    )


def middle_stage(*args):
    return call(
        middle_kernel,
        [(PLANE, BF16)] * 3 + [(PAY, BF16)],
        [
            BUF, BUF, BUF,
            ((2, 3 * C // 2, CELLS), BF16),
            ((2, CELLS, C), F32),
            ((C, C), F32),
            ((4, C, C // 2), F32),
            ((NDEV * 8, C // 2), F32),
        ]
        + [(PLANE, BF16)] * 4,
        80 * TILE,
        *args,
    )


def own_dx_stage(*args):
    return call(own_dx_kernel, [(PLANE, BF16)], [], TILE, *args)[0]


def pair_dx_stage(*args):
    return call(pair_dx_kernel, [(PLANE, BF16)] * 2, [], 2 * TILE, *args)


def first_sum_stage(got):
    return call(first_sum_kernel, [((4, 8, 3 * C // 2), F32)], [], 1000, got)[0]


def sum_stage(*args):
    return call(
        sum_kernel,
        [((2, C), F32), ((2, C), F32), ((TAPS * GW, GW), F32), (PLANE, BF16)],
        [],
        1000,
        *args,
    )


def near_of(plane):
    return plane ^ 1


def far_of(plane):
    return plane - 1 if plane % 2 == 0 else plane + 1


def sent(value, back, partner):
    pipes, planes = lax.axis_size("pipe"), lax.axis_size("sg")
    pairs = [
        (pipe * planes + plane, (pipe - back) * planes + partner(plane))
        for pipe in range(back, pipes)
        for plane in range(planes)
        if 0 <= partner(plane) < planes
    ]
    return lax.ppermute(value, ("pipe", "sg"), pairs)


def per_device(inputs, cotangent, w_in, w_out, w_group):
    shape = inputs.shape
    x = inputs.reshape(PLANE)
    cot = cotangent.reshape(PLANE)
    w_in = w_in.reshape(C, C)
    w_out = w_out.reshape(C, C)
    wg = w_group.reshape(TAPS * GW, C)
    far = sent(x, 0, far_of)
    near = sent(x, 0, near_of)
    kept = [
        pltpu.with_memory_space_constraint(value, pltpu.HBM)
        for value in (x, cot, w_in, w_out, wg)
    ]
    slope1, h1, dh2, wd, z2p, x, cot, w_in = own_stage(*kept)
    own, to_near, to_far, pay = middle_stage(
        near, far, x, cot, w_in, wd, z2p, dh2, h1, slope1
    )
    dx = own_dx_stage(own, cot, w_in)
    part = first_sum_stage(lax.all_to_all(pay, "sg", 0, 0, tiled=True))
    got = lax.all_to_all(part, "dp", 0, 0, tiled=True)
    dx_near, dx_far = pair_dx_stage(to_near, to_far, w_in)
    dx = sent(dx, 1, lambda plane: plane)
    dx_far = sent(dx_far, 1, far_of)
    dx_near = sent(dx_near, 1, near_of)
    grad_in, grad_out, gg, section_grad = sum_stage(got, dx, dx_near, dx_far)
    return (
        section_grad.reshape(shape),
        grad_in[None],
        grad_out[None],
        gg.reshape(1, 3, 3, 3, GW, GW),
    )


def solution(mesh):
    placed = (
        P("pipe", "dp", "sg", None, None, None),
        P("pipe", "dp", "sg", None, None, None),
        P("pipe", None, None),
        P("pipe", None, None),
        P("pipe", None, None, None, None, None),
    )
    return jax.shard_map(
        per_device,
        mesh=mesh,
        in_specs=placed,
        out_specs=(
            P("pipe", "dp", "sg", None, None, None),
            P("pipe", ("dp", "sg"), None),
            P("pipe", ("dp", "sg"), None),
            P("pipe", None, None, None, None, "sg"),
        ),
        check_vma=False,
    )
```

```python
import functools

import jax
import jax.numpy as jnp
from jax import lax
from jax.experimental import pallas as pl
from jax.experimental.pallas import tpu as pltpu
from jax.sharding import PartitionSpec as P

F32 = jnp.float32
BF16 = jnp.bfloat16

C = 256
GW = 8
SIDE = 16
CELLS = SIDE * SIDE
TAPS = 27
PAD_ROWS = CELLS + 2 * SIDE
NDEV = 128
INTERPRET = False

NT = (((1,), (1,)), ((), ()))


def dot(a, b):
    return jnp.dot(a, b, preferred_element_type=F32)


def dot_nt(a, b):
    return lax.dot_general(a, b, NT, preferred_element_type=F32)


def sigmoid(v):
    return 1.0 / (1.0 + jnp.exp(-v))


def column():
    return lax.broadcasted_iota(jnp.int32, (CELLS, C), 0) % SIDE


def fill(buf, plane, sign):
    zeros = jnp.zeros((SIDE, 3 * C), BF16)
    buf[0:SIDE, :] = zeros
    buf[SIDE + CELLS :, :] = zeros
    col = column()
    ahead = jnp.where(col < SIDE - 1, pltpu.roll(plane, CELLS - 1, 0), 0.0)
    behind = jnp.where(col > 0, pltpu.roll(plane, 1, 0), 0.0)
    left, right = (behind, ahead) if sign > 0 else (ahead, behind)
    buf[SIDE : SIDE + CELLS, 0:C] = left.astype(BF16)
    buf[SIDE : SIDE + CELLS, C : 2 * C] = plane.astype(BF16)
    buf[SIDE : SIDE + CELLS, 2 * C :] = right.astype(BF16)


def tap(depth, row, col=0):
    start = ((depth * 3 + row) * 3 + col) * C
    return start if isinstance(start, int) else pl.multiple_of(start, C)


def conv_plane(buf, wd, depth):
    total = None
    for row in range(3):
        term = dot(buf[row * SIDE : row * SIDE + CELLS, :], wd[pl.ds(tap(depth, row), 3 * C), :])
        total = term if total is None else total + term
    return total


def conv_plane_back(buf, wd, depth):
    total = None
    for row in range(3):
        for col in range(3):
            rows = (2 - row) * SIDE
            term = dot_nt(
                buf[rows : rows + CELLS, col * C : (col + 1) * C],
                wd[pl.ds(tap(depth, row, col), C), :],
            )
            total = term if total is None else total + term
    return total


def neighbour_depths():
    odd = lax.axis_index("sg") % 2
    return 2 - 2 * odd, 2 * odd


def activate(x, w_in):
    z1 = dot(x[...], w_in[...])
    sig = sigmoid(z1)
    return (z1 * sig).astype(BF16), sig * (1.0 + z1 * (1.0 - sig))


def far_kernel(far, w_in, wd, z2p, h1, slope, total, buf):
    act, grad = activate(far, w_in)
    slope[...] = grad
    h1[...] = act
    fill(buf, act.astype(F32), 1)
    total[...] = z2p[...] + conv_plane(buf, wd, neighbour_depths()[1])


def spread(wg, wd, which):
    same = (
        lax.broadcasted_iota(jnp.int32, (C, C), 0) // GW
        == lax.broadcasted_iota(jnp.int32, (C, C), 1) // GW
    )
    taps = wg[...].astype(F32)
    for k in which:
        rows = jnp.broadcast_to(taps[k * GW : (k + 1) * GW, :][None], (C // GW, GW, C))
        wd[k * C : (k + 1) * C, :] = jnp.where(same, rows.reshape(C, C), 0.0).astype(BF16)


def own_kernel(
    x_hbm, cot_hbm, w_in_hbm, w_out_hbm, wg_hbm,
    slope1, h1, dh2, wd, z2p, x, cot, w_in,
    buf, w_out, wg, sems,
):
    copies = [
        pltpu.make_async_copy(source, target, sems.at[i])
        for i, (source, target) in enumerate(
            ((wg_hbm, wg), (x_hbm, x), (w_in_hbm, w_in), (cot_hbm, cot), (w_out_hbm, w_out))
        )
    ]
    for copy in copies:
        copy.start()
    copies[0].wait()
    spread(wg, wd, range(TAPS))
    for copy in copies[1:]:
        copy.wait()
    act, grad = activate(x, w_in)
    slope1[...] = grad
    h1[...] = act
    dh2[...] = dot_nt(cot[...], w_out[...]).astype(BF16)
    fill(buf, act.astype(F32), 1)
    z2p[...] = conv_plane(buf, wd, 1)


def middle_kernel(
    near, far, x, cot, w_in, wd, z2f, dh2, h1, slope1, h1f, slopef,
    own, to_near, to_far, pay,
    bufn, buf, ht, slopen, taps, grads, pack,
):
    half = C // 2
    depth_near, depth_far = neighbour_depths()
    act, grad = activate(near, w_in)
    slopen[...] = grad
    fill(bufn, act.astype(F32), 1)
    total = z2f[...] + conv_plane(bufn, wd, depth_near)
    sig = sigmoid(total)
    h2 = (total * sig).astype(BF16)
    slope = sig * (1.0 + total * (1.0 - sig))
    back = (dh2[...].astype(F32) * slope).astype(BF16)
    fill(buf, back.astype(F32), -1)
    outer = dot(h2.T, cot[...])
    for side in range(2):
        grads[2 + side] = outer[:, side * half : (side + 1) * half]
    share = (conv_plane_back(buf, wd, 1) * slope1[...]).astype(BF16)
    own[...] = share
    outer = dot(x[...].T, share)
    for x_next, out, slope, depth in (
        (far, to_far, slopef, depth_far),
        (near, to_near, slopen, depth_near),
    ):
        share = (conv_plane_back(buf, wd, depth) * slope[...]).astype(BF16)
        outer = outer + dot(x_next[...].T, share)
        out[...] = share
    for side in range(2):
        grads[side] = outer[:, side * half : (side + 1) * half]
    for which, plane in enumerate((h1f, h1, None)):
        value = bufn[SIDE : SIDE + CELLS, C : 2 * C] if plane is None else plane[...]
        turned = value.T
        for side in range(2):
            ht[side, which * half : (which + 1) * half, :] = turned[
                side * half : (side + 1) * half, :
            ]
    groups = half // GW
    same = (
        lax.broadcasted_iota(jnp.int32, (half, half), 0) // GW
        == lax.broadcasted_iota(jnp.int32, (half, half), 1) // GW
    )
    taps[TAPS * GW :, :] = jnp.zeros((C - TAPS * GW, C), F32)
    for row in range(3):
        for col in range(3):
            rows = (2 - row) * SIDE
            for side in range(2):
                lanes = col * C + side * half
                full = dot(ht[side], buf[rows : rows + CELLS, lanes : lanes + half])
                for which, depth in enumerate((depth_far, 1, depth_near)):
                    block = jnp.where(same, full[which * half : (which + 1) * half, :], 0.0)
                    first = ((depth * 3 + row) * 3 + col) * GW
                    taps[pl.ds(first, GW), side * half : (side + 1) * half] = jnp.sum(
                        block.reshape(groups, GW, half), axis=0
                    )
    for which in range(2):
        for parity in range(2):
            for side in range(2):
                pack[pl.ds(which * 4 + parity * 2 + side, NDEV, stride=8), :] = grads.at[
                    which * 2 + side
                ][pl.ds(parity, NDEV, stride=2), :]
    blocks = C // GW
    packed = pack[...].reshape(NDEV, 8, half).astype(BF16)
    gg = taps[...].T.reshape(blocks, GW, C).astype(BF16)
    for part in range(NDEV // blocks):
        pay[:, :, part * half : (part + 1) * half] = packed[part * blocks : (part + 1) * blocks]
    pay[:, :, 4 * half :] = gg


def own_dx_kernel(own, cot, w_in, dx):
    dx[...] = (cot[...].astype(F32) + dot_nt(own[...], w_in[...])).astype(BF16)


def pair_dx_kernel(near, far, w_in, dx_near, dx_far):
    dx_near[...] = dot_nt(near[...], w_in[...]).astype(BF16)
    dx_far[...] = dot_nt(far[...], w_in[...]).astype(BF16)


def first_sum_kernel(got, pay):
    total = jnp.sum(got[...].astype(F32), axis=0)
    half = C // 2
    for part in range(4):
        pay[part, :, 0:half] = total[:, part * half : (part + 1) * half]
        pay[part, :, half:] = total[:, 4 * half :]


def sum_kernel(got, dx, dxl, dxr, grad_in, grad_out, gg, section):
    section[...] = (
        dx[...].astype(F32) + (dxl[...].astype(F32) + dxr[...].astype(F32))
    ).astype(BF16)
    total = jnp.sum(got[...].astype(F32), axis=0)
    half = C // 2
    for which, out in enumerate((grad_in, grad_out)):
        for parity in range(2):
            for side in range(2):
                row = which * 4 + parity * 2 + side
                out[parity : parity + 1, side * half : (side + 1) * half] = total[
                    row : row + 1, 0:half
                ]
    gg[...] = total[:, half:].T[0 : TAPS * GW, :]


def call(kernel, outs, scratch, flops, *args, space=pltpu.VMEM):
    shapes = [jax.ShapeDtypeStruct(shape, dtype) for shape, dtype in outs]
    size = sum(a.size * a.dtype.itemsize for a in (*args, *shapes))
    return pl.pallas_call(
        kernel,
        out_shape=shapes,
        in_specs=[pl.BlockSpec(memory_space=space)] * len(args),
        out_specs=[pl.BlockSpec(memory_space=pltpu.VMEM)] * len(outs),
        scratch_shapes=[
            pltpu.VMEM(*entry) if isinstance(entry, tuple) else entry for entry in scratch
        ],
        cost_estimate=pl.CostEstimate(flops=flops, bytes_accessed=size, transcendentals=0),
        compiler_params=pltpu.CompilerParams(vmem_limit_bytes=8 * 1024 * 1024),
        interpret=INTERPRET,
    )(*args)


PLANE = (CELLS, C)
BUF = ((PAD_ROWS, 3 * C), BF16)
PAY = (C // GW, 8, 3 * C)
TILE = 2 * C**3


def own_stage(x, cot, w_in, w_out, wg):
    return call(
        own_kernel,
        [(PLANE, F32), (PLANE, BF16), (PLANE, BF16), ((TAPS * C, C), BF16), (PLANE, F32)]
        + [(PLANE, BF16)] * 3,
        [BUF, (PLANE, BF16), ((TAPS * GW, C), BF16), pltpu.SemaphoreType.DMA((5,))],
        11 * TILE,
        x, cot, w_in, w_out, wg,
        space=pltpu.HBM,
    )


def far_stage(*args):
    return call(
        far_kernel, [(PLANE, BF16), (PLANE, F32), (PLANE, F32)], [BUF], 10 * TILE, *args
    )


def middle_stage(*args):
    return call(
        middle_kernel,
        [(PLANE, BF16)] * 3 + [(PAY, BF16)],
        [
            BUF,
            BUF,
            ((2, 3 * C // 2, CELLS), BF16),
            (PLANE, F32),
            (PLANE, F32),
            ((4, C, C // 2), F32),
            ((NDEV * 8, C // 2), F32),
        ],
        70 * TILE,
        *args,
    )


def own_dx_stage(*args):
    return call(own_dx_kernel, [(PLANE, BF16)], [], TILE, *args)[0]


def pair_dx_stage(*args):
    return call(pair_dx_kernel, [(PLANE, BF16)] * 2, [], 2 * TILE, *args)


def first_sum_stage(got):
    return call(first_sum_kernel, [((4, 8, 3 * C // 2), F32)], [], 1000, got)[0]


def sum_stage(*args):
    return call(
        sum_kernel,
        [((2, C), F32), ((2, C), F32), ((TAPS * GW, GW), F32), (PLANE, BF16)],
        [],
        1000,
        *args,
    )


def near_of(plane):
    return plane ^ 1


def far_of(plane):
    return plane - 1 if plane % 2 == 0 else plane + 1


def sent(value, back, partner):
    pipes, planes = lax.axis_size("pipe"), lax.axis_size("sg")
    pairs = [
        (pipe * planes + plane, (pipe - back) * planes + partner(plane))
        for pipe in range(back, pipes)
        for plane in range(planes)
        if 0 <= partner(plane) < planes
    ]
    return lax.ppermute(value, ("pipe", "sg"), pairs)


def per_device(inputs, cotangent, w_in, w_out, w_group):
    shape = inputs.shape
    x = inputs.reshape(PLANE)
    cot = cotangent.reshape(PLANE)
    w_in = w_in.reshape(C, C)
    w_out = w_out.reshape(C, C)
    wg = w_group.reshape(TAPS * GW, C)
    far = sent(x, 0, far_of)
    near = sent(x, 0, near_of)
    kept = [
        pltpu.with_memory_space_constraint(value, pltpu.HBM)
        for value in (x, cot, w_in, w_out, wg)
    ]
    slope1, h1, dh2, wd, z2p, x, cot, w_in = own_stage(*kept)
    h1f, slopef, z2f = far_stage(far, w_in, wd, z2p)
    own, to_near, to_far, pay = middle_stage(
        near, far, x, cot, w_in, wd, z2f, dh2, h1, slope1, h1f, slopef
    )
    dx = own_dx_stage(own, cot, w_in)
    part = first_sum_stage(lax.all_to_all(pay, "sg", 0, 0, tiled=True))
    got = lax.all_to_all(part, "dp", 0, 0, tiled=True)
    dx_near, dx_far = pair_dx_stage(to_near, to_far, w_in)
    dx = sent(dx, 1, lambda plane: plane)
    dx_far = sent(dx_far, 1, far_of)
    dx_near = sent(dx_near, 1, near_of)
    grad_in, grad_out, gg, section_grad = sum_stage(got, dx, dx_near, dx_far)
    return (
        section_grad.reshape(shape),
        grad_in[None],
        grad_out[None],
        gg.reshape(1, 3, 3, 3, GW, GW),
    )


def solution(mesh):
    placed = (
        P("pipe", "dp", "sg", None, None, None),
        P("pipe", "dp", "sg", None, None, None),
        P("pipe", None, None),
        P("pipe", None, None),
        P("pipe", None, None, None, None, None),
    )
    return jax.shard_map(
        per_device,
        mesh=mesh,
        in_specs=placed,
        out_specs=(
            P("pipe", "dp", "sg", None, None, None),
            P("pipe", ("dp", "sg"), None),
            P("pipe", ("dp", "sg"), None),
            P("pipe", None, None, None, None, "sg"),
        ),
        check_vma=False,
    )
```

```python
import functools

import jax
import jax.numpy as jnp
from jax import lax
from jax.experimental import pallas as pl
from jax.experimental.pallas import tpu as pltpu
from jax.sharding import PartitionSpec as P

F32 = jnp.float32
BF16 = jnp.bfloat16

C = 256
GW = 8
SIDE = 16
CELLS = SIDE * SIDE
TAPS = 27
PAD_ROWS = CELLS + 2 * SIDE
NDEV = 128
INTERPRET = False

NT = (((1,), (1,)), ((), ()))


def dot(a, b):
    return jnp.dot(a, b, preferred_element_type=F32)


def dot_nt(a, b):
    return lax.dot_general(a, b, NT, preferred_element_type=F32)


def sigmoid(v):
    return 1.0 / (1.0 + jnp.exp(-v))


def column():
    return lax.broadcasted_iota(jnp.int32, (CELLS, C), 0) % SIDE


def fill(buf, plane, sign):
    zeros = jnp.zeros((SIDE, 3 * C), BF16)
    buf[0:SIDE, :] = zeros
    buf[SIDE + CELLS :, :] = zeros
    col = column()
    ahead = jnp.where(col < SIDE - 1, pltpu.roll(plane, CELLS - 1, 0), 0.0)
    behind = jnp.where(col > 0, pltpu.roll(plane, 1, 0), 0.0)
    left, right = (behind, ahead) if sign > 0 else (ahead, behind)
    buf[SIDE : SIDE + CELLS, 0:C] = left.astype(BF16)
    buf[SIDE : SIDE + CELLS, C : 2 * C] = plane.astype(BF16)
    buf[SIDE : SIDE + CELLS, 2 * C :] = right.astype(BF16)


def conv_shifted(rows, wd, depth):
    sums = []
    for col in range(3):
        total = None
        for row in range(3):
            term = dot(rows[row * SIDE : row * SIDE + CELLS, :], wd[pl.ds(tap(depth, row, col), C), :])
            total = term if total is None else total + term
        sums.append(total)
    at = column()
    behind = jnp.where(at > 0, pltpu.roll(sums[0], 1, 0), 0.0)
    ahead = jnp.where(at < SIDE - 1, pltpu.roll(sums[2], CELLS - 1, 0), 0.0)
    return sums[1] + (behind + ahead)


def keep_rows(rows, plane):
    zeros = jnp.zeros((SIDE, C), BF16)
    rows[0:SIDE, :] = zeros
    rows[SIDE : SIDE + CELLS, :] = plane
    rows[SIDE + CELLS :, :] = zeros


def tap(depth, row, col=0):
    start = ((depth * 3 + row) * 3 + col) * C
    return start if isinstance(start, int) else pl.multiple_of(start, C)


def conv_plane(buf, wd, depth):
    total = None
    for row in range(3):
        term = dot(buf[row * SIDE : row * SIDE + CELLS, :], wd[pl.ds(tap(depth, row), 3 * C), :])
        total = term if total is None else total + term
    return total


def conv_plane_back(buf, wd, depth):
    total = None
    for row in range(3):
        for col in range(3):
            rows = (2 - row) * SIDE
            term = dot_nt(
                buf[rows : rows + CELLS, col * C : (col + 1) * C],
                wd[pl.ds(tap(depth, row, col), C), :],
            )
            total = term if total is None else total + term
    return total


def neighbour_depths():
    odd = lax.axis_index("sg") % 2
    return 2 - 2 * odd, 2 * odd


def activate(x, w_in):
    z1 = dot(x[...], w_in[...])
    sig = sigmoid(z1)
    return (z1 * sig).astype(BF16), sig * (1.0 + z1 * (1.0 - sig))


def far_kernel(far, w_in, wd, z2p, h1t, slope, total, far_t, buf):
    act, grad = activate(far, w_in)
    slope[...] = grad
    h1t[...] = act.T
    far_t[...] = far[...].T
    keep_rows(buf, act)
    total[...] = z2p[...] + conv_shifted(buf, wd, neighbour_depths()[1])


def spread(wg, wd, which):
    same = (
        lax.broadcasted_iota(jnp.int32, (C, C), 0) // GW
        == lax.broadcasted_iota(jnp.int32, (C, C), 1) // GW
    )
    taps = wg[...].astype(F32)
    for k in which:
        rows = jnp.broadcast_to(taps[k * GW : (k + 1) * GW, :][None], (C // GW, GW, C))
        wd[k * C : (k + 1) * C, :] = jnp.where(same, rows.reshape(C, C), 0.0).astype(BF16)


def own_kernel(
    x_hbm, cot_hbm, w_in_hbm, w_out_hbm, wg_hbm,
    slope1, h1t, dh2, wd, z2p, xt, cot, w_in,
    x, buf, w_out, wg, sems,
):
    copies = [
        pltpu.make_async_copy(source, target, sems.at[i])
        for i, (source, target) in enumerate(
            ((wg_hbm, wg), (x_hbm, x), (w_in_hbm, w_in), (cot_hbm, cot), (w_out_hbm, w_out))
        )
    ]
    for copy in copies:
        copy.start()
    copies[0].wait()
    spread(wg, wd, range(TAPS))
    for copy in copies[1:]:
        copy.wait()
    act, grad = activate(x, w_in)
    slope1[...] = grad
    h1t[...] = act.T
    xt[...] = x[...].T
    dh2[...] = dot_nt(cot[...], w_out[...]).astype(BF16)
    keep_rows(buf, act)
    z2p[...] = conv_shifted(buf, wd, 1)


def middle_kernel(
    near, far_t, xt, cot, w_in, wd, z2f, dh2, h1t, slope1, h1ft, slopef,
    own, to_near, to_far, pay,
    bufn, buf, ht, slopen, taps, grads, pack,
):
    half = C // 2
    depth_near, depth_far = neighbour_depths()
    act, grad = activate(near, w_in)
    slopen[...] = grad
    keep_rows(bufn, act)
    total = z2f[...] + conv_shifted(bufn, wd, depth_near)
    sig = sigmoid(total)
    h2 = (total * sig).astype(BF16)
    slope = sig * (1.0 + total * (1.0 - sig))
    back = (dh2[...].astype(F32) * slope).astype(BF16)
    fill(buf, back.astype(F32), -1)
    outer = dot(h2.T, cot[...])
    for side in range(2):
        grads[2 + side] = outer[:, side * half : (side + 1) * half]
    share = (conv_plane_back(buf, wd, 1) * slope1[...]).astype(BF16)
    own[...] = share
    outer = dot(xt[...], share)
    for turned, out, slope, depth in (
        (far_t[...], to_far, slopef, depth_far),
        (near[...].T, to_near, slopen, depth_near),
    ):
        share = (conv_plane_back(buf, wd, depth) * slope[...]).astype(BF16)
        outer = outer + dot(turned, share)
        out[...] = share
    for side in range(2):
        grads[side] = outer[:, side * half : (side + 1) * half]
    for which, turned in enumerate((h1ft[...], h1t[...], act.T)):
        for side in range(2):
            ht[side, which * half : (which + 1) * half, :] = turned[
                side * half : (side + 1) * half, :
            ]
    groups = half // GW
    same = (
        lax.broadcasted_iota(jnp.int32, (half, half), 0) // GW
        == lax.broadcasted_iota(jnp.int32, (half, half), 1) // GW
    )
    taps[TAPS * GW :, :] = jnp.zeros((C - TAPS * GW, C), F32)
    for row in range(3):
        rows = (2 - row) * SIDE
        for side in range(2):
            wide = jnp.concatenate(
                [
                    buf[rows : rows + CELLS, col * C + side * half : col * C + (side + 1) * half]
                    for col in range(3)
                ],
                axis=1,
            )
            full = dot(ht[side], wide)
            for col in range(3):
                for which, depth in enumerate((depth_far, 1, depth_near)):
                    block = jnp.where(
                        same,
                        full[which * half : (which + 1) * half, col * half : (col + 1) * half],
                        0.0,
                    )
                    first = ((depth * 3 + row) * 3 + col) * GW
                    taps[pl.ds(first, GW), side * half : (side + 1) * half] = jnp.sum(
                        block.reshape(groups, GW, half), axis=0
                    )
    for which in range(2):
        for parity in range(2):
            for side in range(2):
                pack[pl.ds(which * 4 + parity * 2 + side, NDEV, stride=8), :] = grads.at[
                    which * 2 + side
                ][pl.ds(parity, NDEV, stride=2), :]
    blocks = C // GW
    packed = pack[...].reshape(NDEV, 8, half).astype(BF16)
    gg = taps[...].T.reshape(blocks, GW, C).astype(BF16)
    for part in range(NDEV // blocks):
        pay[:, :, part * half : (part + 1) * half] = packed[part * blocks : (part + 1) * blocks]
    pay[:, :, 4 * half :] = gg


def own_dx_kernel(own, cot, w_in, dx):
    dx[...] = (cot[...].astype(F32) + dot_nt(own[...], w_in[...])).astype(BF16)


def pair_dx_kernel(near, far, w_in, dx_near, dx_far):
    dx_near[...] = dot_nt(near[...], w_in[...]).astype(BF16)
    dx_far[...] = dot_nt(far[...], w_in[...]).astype(BF16)


def first_sum_kernel(got, pay):
    total = jnp.sum(got[...].astype(F32), axis=0)
    half = C // 2
    for part in range(4):
        pay[part, :, 0:half] = total[:, part * half : (part + 1) * half]
        pay[part, :, half:] = total[:, 4 * half :]


def sum_kernel(got, dx, dxl, dxr, grad_in, grad_out, gg, section):
    section[...] = (
        dx[...].astype(F32) + (dxl[...].astype(F32) + dxr[...].astype(F32))
    ).astype(BF16)
    total = jnp.sum(got[...].astype(F32), axis=0)
    half = C // 2
    for which, out in enumerate((grad_in, grad_out)):
        for parity in range(2):
            for side in range(2):
                row = which * 4 + parity * 2 + side
                out[parity : parity + 1, side * half : (side + 1) * half] = total[
                    row : row + 1, 0:half
                ]
    gg[...] = total[:, half:].T[0 : TAPS * GW, :]


def call(kernel, outs, scratch, flops, *args, space=pltpu.VMEM):
    shapes = [jax.ShapeDtypeStruct(shape, dtype) for shape, dtype in outs]
    size = sum(a.size * a.dtype.itemsize for a in (*args, *shapes))
    return pl.pallas_call(
        kernel,
        out_shape=shapes,
        in_specs=[pl.BlockSpec(memory_space=space)] * len(args),
        out_specs=[pl.BlockSpec(memory_space=pltpu.VMEM)] * len(outs),
        scratch_shapes=[
            pltpu.VMEM(*entry) if isinstance(entry, tuple) else entry for entry in scratch
        ],
        cost_estimate=pl.CostEstimate(flops=flops, bytes_accessed=size, transcendentals=0),
        compiler_params=pltpu.CompilerParams(vmem_limit_bytes=8 * 1024 * 1024),
        interpret=INTERPRET,
    )(*args)


PLANE = (CELLS, C)
BUF = ((PAD_ROWS, 3 * C), BF16)
PAY = (C // GW, 8, 3 * C)
TILE = 2 * C**3


def own_stage(x, cot, w_in, w_out, wg):
    return call(
        own_kernel,
        [(PLANE, F32), (PLANE, BF16), (PLANE, BF16), ((TAPS * C, C), BF16), (PLANE, F32)]
        + [(PLANE, BF16)] * 3,
        [(PLANE, BF16), ((PAD_ROWS, C), BF16), (PLANE, BF16), ((TAPS * GW, C), BF16), pltpu.SemaphoreType.DMA((5,))],
        11 * TILE,
        x, cot, w_in, w_out, wg,
        space=pltpu.HBM,
    )


def far_stage(*args):
    return call(
        far_kernel, [(PLANE, BF16), (PLANE, F32), (PLANE, F32), (PLANE, BF16)], [((PAD_ROWS, C), BF16)], 10 * TILE, *args
    )


def middle_stage(*args):
    return call(
        middle_kernel,
        [(PLANE, BF16)] * 3 + [(PAY, BF16)],
        [
            ((PAD_ROWS, C), BF16),
            BUF,
            ((2, 3 * C // 2, CELLS), BF16),
            (PLANE, F32),
            (PLANE, F32),
            ((4, C, C // 2), F32),
            ((NDEV * 8, C // 2), F32),
        ],
        70 * TILE,
        *args,
    )


def own_dx_stage(*args):
    return call(own_dx_kernel, [(PLANE, BF16)], [], TILE, *args)[0]


def pair_dx_stage(*args):
    return call(pair_dx_kernel, [(PLANE, BF16)] * 2, [], 2 * TILE, *args)


def first_sum_stage(got):
    return call(first_sum_kernel, [((4, 8, 3 * C // 2), F32)], [], 1000, got)[0]


def sum_stage(*args):
    return call(
        sum_kernel,
        [((2, C), F32), ((2, C), F32), ((TAPS * GW, GW), F32), (PLANE, BF16)],
        [],
        1000,
        *args,
    )


def near_of(plane):
    return plane ^ 1


def far_of(plane):
    return plane - 1 if plane % 2 == 0 else plane + 1


def sent(value, back, partner):
    pipes, planes = lax.axis_size("pipe"), lax.axis_size("sg")
    pairs = [
        (pipe * planes + plane, (pipe - back) * planes + partner(plane))
        for pipe in range(back, pipes)
        for plane in range(planes)
        if 0 <= partner(plane) < planes
    ]
    return lax.ppermute(value, ("pipe", "sg"), pairs)


def per_device(inputs, cotangent, w_in, w_out, w_group):
    shape = inputs.shape
    x = inputs.reshape(PLANE)
    cot = cotangent.reshape(PLANE)
    w_in = w_in.reshape(C, C)
    w_out = w_out.reshape(C, C)
    wg = w_group.reshape(TAPS * GW, C)
    far = sent(x, 0, far_of)
    near = sent(x, 0, near_of)
    kept = [
        pltpu.with_memory_space_constraint(value, pltpu.HBM)
        for value in (x, cot, w_in, w_out, wg)
    ]
    slope1, h1t, dh2, wd, z2p, xt, cot, w_in = own_stage(*kept)
    h1ft, slopef, z2f, far_t = far_stage(far, w_in, wd, z2p)
    own, to_near, to_far, pay = middle_stage(
        near, far_t, xt, cot, w_in, wd, z2f, dh2, h1t, slope1, h1ft, slopef
    )
    dx = own_dx_stage(own, cot, w_in)
    part = first_sum_stage(lax.all_to_all(pay, "sg", 0, 0, tiled=True))
    got = lax.all_to_all(part, "dp", 0, 0, tiled=True)
    dx_near, dx_far = pair_dx_stage(to_near, to_far, w_in)
    dx = sent(dx, 1, lambda plane: plane)
    dx_far = sent(dx_far, 1, far_of)
    dx_near = sent(dx_near, 1, near_of)
    grad_in, grad_out, gg, section_grad = sum_stage(got, dx, dx_near, dx_far)
    return (
        section_grad.reshape(shape),
        grad_in[None],
        grad_out[None],
        gg.reshape(1, 3, 3, 3, GW, GW),
    )


def solution(mesh):
    placed = (
        P("pipe", "dp", "sg", None, None, None),
        P("pipe", "dp", "sg", None, None, None),
        P("pipe", None, None),
        P("pipe", None, None),
        P("pipe", None, None, None, None, None),
    )
    return jax.shard_map(
        per_device,
        mesh=mesh,
        in_specs=placed,
        out_specs=(
            P("pipe", "dp", "sg", None, None, None),
            P("pipe", ("dp", "sg"), None),
            P("pipe", ("dp", "sg"), None),
            P("pipe", None, None, None, None, "sg"),
        ),
        check_vma=False,
    )
```

```python
import functools

import jax
import jax.numpy as jnp
from jax import lax
from jax.experimental import pallas as pl
from jax.experimental.pallas import tpu as pltpu
from jax.sharding import PartitionSpec as P

F32 = jnp.float32
BF16 = jnp.bfloat16

C = 256
GW = 8
SIDE = 16
CELLS = SIDE * SIDE
TAPS = 27
PAD_ROWS = CELLS + 2 * SIDE
NDEV = 128
INTERPRET = False
SAMPLE_ORDER = [3, 2, 1, 0]
ORDER = list(range(C // GW - 1, -1, -1))

NT = (((1,), (1,)), ((), ()))


def dot(a, b):
    return jnp.dot(a, b, preferred_element_type=F32)


def dot_nt(a, b):
    return lax.dot_general(a, b, NT, preferred_element_type=F32)


def sigmoid(v):
    return 1.0 / (1.0 + jnp.exp(-v))


def column():
    return lax.broadcasted_iota(jnp.int32, (CELLS, C), 0) % SIDE


def fill(buf, plane, sign):
    zeros = jnp.zeros((SIDE, 3 * C), BF16)
    buf[0:SIDE, :] = zeros
    buf[SIDE + CELLS :, :] = zeros
    col = column()
    ahead = jnp.where(col < SIDE - 1, pltpu.roll(plane, CELLS - 1, 0), 0.0)
    behind = jnp.where(col > 0, pltpu.roll(plane, 1, 0), 0.0)
    left, right = (behind, ahead) if sign > 0 else (ahead, behind)
    buf[SIDE : SIDE + CELLS, 0:C] = left.astype(BF16)
    buf[SIDE : SIDE + CELLS, C : 2 * C] = plane.astype(BF16)
    buf[SIDE : SIDE + CELLS, 2 * C :] = right.astype(BF16)


def conv_shifted(rows, wd, depth):
    sums = []
    for col in range(3):
        total = None
        for row in range(3):
            term = dot(rows[row * SIDE : row * SIDE + CELLS, :], wd[pl.ds(tap(depth, row, col), C), :])
            total = term if total is None else total + term
        sums.append(total)
    at = column()
    behind = jnp.where(at > 0, pltpu.roll(sums[0], 1, 0), 0.0)
    ahead = jnp.where(at < SIDE - 1, pltpu.roll(sums[2], CELLS - 1, 0), 0.0)
    return sums[1] + (behind + ahead)


def keep_rows(rows, plane):
    zeros = jnp.zeros((SIDE, C), BF16)
    rows[0:SIDE, :] = zeros
    rows[SIDE : SIDE + CELLS, :] = plane
    rows[SIDE + CELLS :, :] = zeros


def tap(depth, row, col=0):
    start = ((depth * 3 + row) * 3 + col) * C
    return start if isinstance(start, int) else pl.multiple_of(start, C)


def conv_plane(buf, wd, depth):
    total = None
    for row in range(3):
        term = dot(buf[row * SIDE : row * SIDE + CELLS, :], wd[pl.ds(tap(depth, row), 3 * C), :])
        total = term if total is None else total + term
    return total


def conv_plane_back(buf, wd, depth):
    total = None
    for row in range(3):
        for col in range(3):
            rows = (2 - row) * SIDE
            term = dot_nt(
                buf[rows : rows + CELLS, col * C : (col + 1) * C],
                wd[pl.ds(tap(depth, row, col), C), :],
            )
            total = term if total is None else total + term
    return total


def neighbour_depths():
    odd = lax.axis_index("sg") % 2
    return 2 - 2 * odd, 2 * odd


def activate(x, w_in):
    z1 = dot(x[...], w_in[...])
    sig = sigmoid(z1)
    return (z1 * sig).astype(BF16), sig * (1.0 + z1 * (1.0 - sig))


def far_kernel(far, w_in, wd, z2p, h1t, slope, total, far_t, buf):
    act, grad = activate(far, w_in)
    slope[...] = grad
    h1t[...] = act.T
    far_t[...] = far[...].T
    keep_rows(buf, act)
    total[...] = z2p[...] + conv_shifted(buf, wd, neighbour_depths()[1])


def spread(wg, wd, which):
    same = (
        lax.broadcasted_iota(jnp.int32, (C, C), 0) // GW
        == lax.broadcasted_iota(jnp.int32, (C, C), 1) // GW
    )
    taps = wg[...].astype(F32)
    for k in which:
        rows = jnp.broadcast_to(taps[k * GW : (k + 1) * GW, :][None], (C // GW, GW, C))
        wd[k * C : (k + 1) * C, :] = jnp.where(same, rows.reshape(C, C), 0.0).astype(BF16)


def own_kernel(
    x_hbm, cot_hbm, w_in_hbm, w_out_hbm, wg_hbm,
    slope1, h1t, dh2, wd, z2p, xt, cot, w_in,
    x, buf, w_out, wg, sems,
):
    copies = [
        pltpu.make_async_copy(source, target, sems.at[i])
        for i, (source, target) in enumerate(
            ((wg_hbm, wg), (x_hbm, x), (w_in_hbm, w_in), (cot_hbm, cot), (w_out_hbm, w_out))
        )
    ]
    for copy in copies:
        copy.start()
    copies[0].wait()
    spread(wg, wd, range(TAPS))
    for copy in copies[1:]:
        copy.wait()
    act, grad = activate(x, w_in)
    slope1[...] = grad
    h1t[...] = act.T
    xt[...] = x[...].T
    dh2[...] = dot_nt(cot[...], w_out[...]).astype(BF16)
    keep_rows(buf, act)
    z2p[...] = conv_shifted(buf, wd, 1)


def middle_kernel(
    near, far_t, xt, cot, w_in, wd, z2f, dh2, h1t, slope1, h1ft, slopef,
    own, to_near, to_far, pay,
    bufn, buf, ht, slopen, taps, grads, pack,
):
    half = C // 2
    depth_near, depth_far = neighbour_depths()
    act, grad = activate(near, w_in)
    slopen[...] = grad
    keep_rows(bufn, act)
    total = z2f[...] + conv_shifted(bufn, wd, depth_near)
    sig = sigmoid(total)
    h2 = (total * sig).astype(BF16)
    slope = sig * (1.0 + total * (1.0 - sig))
    back = (dh2[...].astype(F32) * slope).astype(BF16)
    fill(buf, back.astype(F32), -1)
    outer = dot(h2.T, cot[...])
    for side in range(2):
        grads[2 + side] = outer[:, side * half : (side + 1) * half]
    share = (conv_plane_back(buf, wd, 1) * slope1[...]).astype(BF16)
    own[...] = share
    outer = dot(xt[...], share)
    for turned, out, slope, depth in (
        (far_t[...], to_far, slopef, depth_far),
        (near[...].T, to_near, slopen, depth_near),
    ):
        share = (conv_plane_back(buf, wd, depth) * slope[...]).astype(BF16)
        outer = outer + dot(turned, share)
        out[...] = share
    for side in range(2):
        grads[side] = outer[:, side * half : (side + 1) * half]
    for which, turned in enumerate((h1ft[...], h1t[...], act.T)):
        for side in range(2):
            ht[side, which * half : (which + 1) * half, :] = turned[
                side * half : (side + 1) * half, :
            ]
    groups = half // GW
    same = (
        lax.broadcasted_iota(jnp.int32, (half, half), 0) // GW
        == lax.broadcasted_iota(jnp.int32, (half, half), 1) // GW
    )
    taps[TAPS * GW :, :] = jnp.zeros((C - TAPS * GW, C), F32)
    for row in range(3):
        rows = (2 - row) * SIDE
        for side in range(2):
            wide = jnp.concatenate(
                [
                    buf[rows : rows + CELLS, col * C + side * half : col * C + (side + 1) * half]
                    for col in range(3)
                ],
                axis=1,
            )
            full = dot(ht[side], wide)
            for col in range(3):
                for which, depth in enumerate((depth_far, 1, depth_near)):
                    block = jnp.where(
                        same,
                        full[which * half : (which + 1) * half, col * half : (col + 1) * half],
                        0.0,
                    )
                    first = ((depth * 3 + row) * 3 + col) * GW
                    taps[pl.ds(first, GW), side * half : (side + 1) * half] = jnp.sum(
                        block.reshape(groups, GW, half), axis=0
                    )
    for which in range(2):
        for parity in range(2):
            for side in range(2):
                pack[pl.ds(which * 4 + parity * 2 + side, NDEV, stride=8), :] = grads.at[
                    which * 2 + side
                ][pl.ds(parity, NDEV, stride=2), :]
    blocks = C // GW
    packed = pack[...].reshape(NDEV, 8, half).astype(BF16)
    gg = taps[...].T.reshape(blocks, GW, C).astype(BF16)
    for at, plane in enumerate(ORDER):
        for part in range(NDEV // blocks):
            pay[at, :, part * half : (part + 1) * half] = packed[part * blocks + plane]
        pay[at, :, 4 * half :] = gg[plane]


def own_dx_kernel(own, cot, w_in, dx):
    dx[...] = (cot[...].astype(F32) + dot_nt(own[...], w_in[...])).astype(BF16)


def pair_dx_kernel(near, far, w_in, dx_near, dx_far):
    dx_near[...] = dot_nt(near[...], w_in[...]).astype(BF16)
    dx_far[...] = dot_nt(far[...], w_in[...]).astype(BF16)


def first_sum_kernel(got, pay):
    total = jnp.sum(got[...].astype(F32), axis=0)
    half = C // 2
    for at, part in enumerate(SAMPLE_ORDER):
        pay[at, :, 0:half] = total[:, part * half : (part + 1) * half]
        pay[at, :, half:] = total[:, 4 * half :]


def sum_kernel(got, dx, dxl, dxr, grad_in, grad_out, gg, section):
    section[...] = (
        dx[...].astype(F32) + (dxl[...].astype(F32) + dxr[...].astype(F32))
    ).astype(BF16)
    total = jnp.sum(got[...].astype(F32), axis=0)
    half = C // 2
    for which, out in enumerate((grad_in, grad_out)):
        for parity in range(2):
            for side in range(2):
                row = which * 4 + parity * 2 + side
                out[parity : parity + 1, side * half : (side + 1) * half] = total[
                    row : row + 1, 0:half
                ]
    gg[...] = total[:, half:].T[0 : TAPS * GW, :]


def call(kernel, outs, scratch, flops, *args, space=pltpu.VMEM):
    shapes = [jax.ShapeDtypeStruct(shape, dtype) for shape, dtype in outs]
    size = sum(a.size * a.dtype.itemsize for a in (*args, *shapes))
    return pl.pallas_call(
        kernel,
        out_shape=shapes,
        in_specs=[pl.BlockSpec(memory_space=space)] * len(args),
        out_specs=[pl.BlockSpec(memory_space=pltpu.VMEM)] * len(outs),
        scratch_shapes=[
            pltpu.VMEM(*entry) if isinstance(entry, tuple) else entry for entry in scratch
        ],
        cost_estimate=pl.CostEstimate(flops=flops, bytes_accessed=size, transcendentals=0),
        compiler_params=pltpu.CompilerParams(vmem_limit_bytes=8 * 1024 * 1024),
        interpret=INTERPRET,
    )(*args)


PLANE = (CELLS, C)
BUF = ((PAD_ROWS, 3 * C), BF16)
PAY = (C // GW, 8, 3 * C)
TILE = 2 * C**3


def own_stage(x, cot, w_in, w_out, wg):
    return call(
        own_kernel,
        [(PLANE, F32), (PLANE, BF16), (PLANE, BF16), ((TAPS * C, C), BF16), (PLANE, F32)]
        + [(PLANE, BF16)] * 3,
        [(PLANE, BF16), ((PAD_ROWS, C), BF16), (PLANE, BF16), ((TAPS * GW, C), BF16), pltpu.SemaphoreType.DMA((5,))],
        11 * TILE,
        x, cot, w_in, w_out, wg,
        space=pltpu.HBM,
    )


def far_stage(*args):
    return call(
        far_kernel, [(PLANE, BF16), (PLANE, F32), (PLANE, F32), (PLANE, BF16)], [((PAD_ROWS, C), BF16)], 10 * TILE, *args
    )


def middle_stage(*args):
    return call(
        middle_kernel,
        [(PLANE, BF16)] * 3 + [(PAY, BF16)],
        [
            ((PAD_ROWS, C), BF16),
            BUF,
            ((2, 3 * C // 2, CELLS), BF16),
            (PLANE, F32),
            (PLANE, F32),
            ((4, C, C // 2), F32),
            ((NDEV * 8, C // 2), F32),
        ],
        70 * TILE,
        *args,
    )


def own_dx_stage(*args):
    return call(own_dx_kernel, [(PLANE, BF16)], [], TILE, *args)[0]


def pair_dx_stage(*args):
    return call(pair_dx_kernel, [(PLANE, BF16)] * 2, [], 2 * TILE, *args)


def first_sum_stage(got):
    return call(first_sum_kernel, [((4, 8, 3 * C // 2), F32)], [], 1000, got)[0]


def sum_stage(*args):
    return call(
        sum_kernel,
        [((2, C), F32), ((2, C), F32), ((TAPS * GW, GW), F32), (PLANE, BF16)],
        [],
        1000,
        *args,
    )


def near_of(plane):
    return plane ^ 1


def far_of(plane):
    return plane - 1 if plane % 2 == 0 else plane + 1


def sent(value, back, partner):
    pipes, planes = lax.axis_size("pipe"), lax.axis_size("sg")
    pairs = [
        (pipe * planes + plane, (pipe - back) * planes + partner(plane))
        for pipe in range(back, pipes)
        for plane in range(planes)
        if 0 <= partner(plane) < planes
    ]
    return lax.ppermute(value, ("pipe", "sg"), pairs)


def per_device(inputs, cotangent, w_in, w_out, w_group):
    shape = inputs.shape
    x = inputs.reshape(PLANE)
    cot = cotangent.reshape(PLANE)
    w_in = w_in.reshape(C, C)
    w_out = w_out.reshape(C, C)
    wg = w_group.reshape(TAPS * GW, C)
    far = sent(x, 0, far_of)
    near = sent(x, 0, near_of)
    kept = [
        pltpu.with_memory_space_constraint(value, pltpu.HBM)
        for value in (x, cot, w_in, w_out, wg)
    ]
    slope1, h1t, dh2, wd, z2p, xt, cot, w_in = own_stage(*kept)
    h1ft, slopef, z2f, far_t = far_stage(far, w_in, wd, z2p)
    own, to_near, to_far, pay = middle_stage(
        near, far_t, xt, cot, w_in, wd, z2f, dh2, h1t, slope1, h1ft, slopef
    )
    dx = own_dx_stage(own, cot, w_in)
    part = first_sum_stage(lax.all_to_all(pay, "sg", 0, 0, tiled=True, axis_index_groups=[ORDER]))
    got = lax.all_to_all(
        part, "dp", 0, 0, tiled=True, axis_index_groups=[SAMPLE_ORDER]
    )
    dx_near, dx_far = pair_dx_stage(to_near, to_far, w_in)
    dx = sent(dx, 1, lambda plane: plane)
    dx_far = sent(dx_far, 1, far_of)
    dx_near = sent(dx_near, 1, near_of)
    grad_in, grad_out, gg, section_grad = sum_stage(got, dx, dx_near, dx_far)
    return (
        section_grad.reshape(shape),
        grad_in[None],
        grad_out[None],
        gg.reshape(1, 3, 3, 3, GW, GW),
    )


def solution(mesh):
    placed = (
        P("pipe", "dp", "sg", None, None, None),
        P("pipe", "dp", "sg", None, None, None),
        P("pipe", None, None),
        P("pipe", None, None),
        P("pipe", None, None, None, None, None),
    )
    return jax.shard_map(
        per_device,
        mesh=mesh,
        in_specs=placed,
        out_specs=(
            P("pipe", "dp", "sg", None, None, None),
            P("pipe", ("dp", "sg"), None),
            P("pipe", ("dp", "sg"), None),
            P("pipe", None, None, None, None, "sg"),
        ),
        check_vma=False,
    )
```

```python
import functools

import jax
import jax.numpy as jnp
from jax import lax
from jax.experimental import pallas as pl
from jax.experimental.pallas import tpu as pltpu
from jax.sharding import PartitionSpec as P

F32 = jnp.float32
BF16 = jnp.bfloat16

C = 256
GW = 8
SIDE = 16
CELLS = SIDE * SIDE
TAPS = 27
PAD_ROWS = CELLS + 2 * SIDE
NDEV = 128
INTERPRET = False
SAMPLE_ORDER = [2, 3, 0, 1]
ORDER = [(20 - step) % (C // GW) for step in range(C // GW)]

NT = (((1,), (1,)), ((), ()))


def dot(a, b):
    return jnp.dot(a, b, preferred_element_type=F32)


def dot_nt(a, b):
    return lax.dot_general(a, b, NT, preferred_element_type=F32)


def sigmoid(v):
    return 1.0 / (1.0 + jnp.exp(-v))


def column():
    return lax.broadcasted_iota(jnp.int32, (CELLS, C), 0) % SIDE


def fill(buf, plane, sign):
    zeros = jnp.zeros((SIDE, 3 * C), BF16)
    buf[0:SIDE, :] = zeros
    buf[SIDE + CELLS :, :] = zeros
    col = column()
    ahead = jnp.where(col < SIDE - 1, pltpu.roll(plane, CELLS - 1, 0), 0.0)
    behind = jnp.where(col > 0, pltpu.roll(plane, 1, 0), 0.0)
    left, right = (behind, ahead) if sign > 0 else (ahead, behind)
    buf[SIDE : SIDE + CELLS, 0:C] = left.astype(BF16)
    buf[SIDE : SIDE + CELLS, C : 2 * C] = plane.astype(BF16)
    buf[SIDE : SIDE + CELLS, 2 * C :] = right.astype(BF16)


def conv_shifted(rows, wd, depth):
    sums = []
    for col in range(3):
        total = None
        for row in range(3):
            term = dot(rows[row * SIDE : row * SIDE + CELLS, :], wd[pl.ds(tap(depth, row, col), C), :])
            total = term if total is None else total + term
        sums.append(total)
    at = column()
    behind = jnp.where(at > 0, pltpu.roll(sums[0], 1, 0), 0.0)
    ahead = jnp.where(at < SIDE - 1, pltpu.roll(sums[2], CELLS - 1, 0), 0.0)
    return sums[1] + (behind + ahead)


def keep_rows(rows, plane):
    zeros = jnp.zeros((SIDE, C), BF16)
    rows[0:SIDE, :] = zeros
    rows[SIDE : SIDE + CELLS, :] = plane
    rows[SIDE + CELLS :, :] = zeros


def tap(depth, row, col=0):
    start = ((depth * 3 + row) * 3 + col) * C
    return start if isinstance(start, int) else pl.multiple_of(start, C)


def conv_plane(buf, wd, depth):
    total = None
    for row in range(3):
        term = dot(buf[row * SIDE : row * SIDE + CELLS, :], wd[pl.ds(tap(depth, row), 3 * C), :])
        total = term if total is None else total + term
    return total


def conv_plane_back(buf, wd, depth):
    total = None
    for row in range(3):
        for col in range(3):
            rows = (2 - row) * SIDE
            term = dot_nt(
                buf[rows : rows + CELLS, col * C : (col + 1) * C],
                wd[pl.ds(tap(depth, row, col), C), :],
            )
            total = term if total is None else total + term
    return total


def neighbour_depths():
    odd = lax.axis_index("sg") % 2
    return 2 - 2 * odd, 2 * odd


def activate(x, w_in):
    z1 = dot(x[...], w_in[...])
    sig = sigmoid(z1)
    return (z1 * sig).astype(BF16), sig * (1.0 + z1 * (1.0 - sig))


def far_kernel(far, w_in, wd, z2p, h1t, slope, total, far_t, buf):
    act, grad = activate(far, w_in)
    slope[...] = grad
    h1t[...] = act.T
    far_t[...] = far[...].T
    keep_rows(buf, act)
    total[...] = z2p[...] + conv_shifted(buf, wd, neighbour_depths()[1])


def spread(wg, wd, which):
    same = (
        lax.broadcasted_iota(jnp.int32, (C, C), 0) // GW
        == lax.broadcasted_iota(jnp.int32, (C, C), 1) // GW
    )
    taps = wg[...].astype(F32)
    for k in which:
        rows = jnp.broadcast_to(taps[k * GW : (k + 1) * GW, :][None], (C // GW, GW, C))
        wd[k * C : (k + 1) * C, :] = jnp.where(same, rows.reshape(C, C), 0.0).astype(BF16)


def own_kernel(
    x_hbm, cot_hbm, w_in_hbm, w_out_hbm, wg_hbm,
    slope1, h1t, dh2, wd, z2p, xt, cot, w_in,
    x, buf, w_out, wg, sems,
):
    copies = [
        pltpu.make_async_copy(source, target, sems.at[i])
        for i, (source, target) in enumerate(
            ((wg_hbm, wg), (x_hbm, x), (w_in_hbm, w_in), (cot_hbm, cot), (w_out_hbm, w_out))
        )
    ]
    for copy in copies:
        copy.start()
    copies[0].wait()
    spread(wg, wd, range(TAPS))
    for copy in copies[1:]:
        copy.wait()
    act, grad = activate(x, w_in)
    slope1[...] = grad
    h1t[...] = act.T
    xt[...] = x[...].T
    dh2[...] = dot_nt(cot[...], w_out[...]).astype(BF16)
    keep_rows(buf, act)
    z2p[...] = conv_shifted(buf, wd, 1)


def middle_kernel(
    near, far_t, xt, cot, w_in, wd, z2f, dh2, h1t, slope1, h1ft, slopef,
    own, to_near, to_far, pay,
    bufn, buf, ht, slopen, taps, grads, pack,
):
    half = C // 2
    depth_near, depth_far = neighbour_depths()
    act, grad = activate(near, w_in)
    slopen[...] = grad
    keep_rows(bufn, act)
    total = z2f[...] + conv_shifted(bufn, wd, depth_near)
    sig = sigmoid(total)
    h2 = (total * sig).astype(BF16)
    slope = sig * (1.0 + total * (1.0 - sig))
    back = (dh2[...].astype(F32) * slope).astype(BF16)
    fill(buf, back.astype(F32), -1)
    outer = dot(h2.T, cot[...])
    for side in range(2):
        grads[2 + side] = outer[:, side * half : (side + 1) * half]
    share = (conv_plane_back(buf, wd, 1) * slope1[...]).astype(BF16)
    own[...] = share
    outer = dot(xt[...], share)
    for turned, out, slope, depth in (
        (far_t[...], to_far, slopef, depth_far),
        (near[...].T, to_near, slopen, depth_near),
    ):
        share = (conv_plane_back(buf, wd, depth) * slope[...]).astype(BF16)
        outer = outer + dot(turned, share)
        out[...] = share
    for side in range(2):
        grads[side] = outer[:, side * half : (side + 1) * half]
    for which, turned in enumerate((h1ft[...], h1t[...], act.T)):
        for side in range(2):
            ht[side, which * half : (which + 1) * half, :] = turned[
                side * half : (side + 1) * half, :
            ]
    groups = half // GW
    same = (
        lax.broadcasted_iota(jnp.int32, (half, half), 0) // GW
        == lax.broadcasted_iota(jnp.int32, (half, half), 1) // GW
    )
    taps[TAPS * GW :, :] = jnp.zeros((C - TAPS * GW, C), F32)
    for row in range(3):
        rows = (2 - row) * SIDE
        for side in range(2):
            wide = jnp.concatenate(
                [
                    buf[rows : rows + CELLS, col * C + side * half : col * C + (side + 1) * half]
                    for col in range(3)
                ],
                axis=1,
            )
            full = dot(ht[side], wide)
            for col in range(3):
                for which, depth in enumerate((depth_far, 1, depth_near)):
                    block = jnp.where(
                        same,
                        full[which * half : (which + 1) * half, col * half : (col + 1) * half],
                        0.0,
                    )
                    first = ((depth * 3 + row) * 3 + col) * GW
                    taps[pl.ds(first, GW), side * half : (side + 1) * half] = jnp.sum(
                        block.reshape(groups, GW, half), axis=0
                    )
    for which in range(2):
        for parity in range(2):
            for side in range(2):
                pack[pl.ds(which * 4 + parity * 2 + side, NDEV, stride=8), :] = grads.at[
                    which * 2 + side
                ][pl.ds(parity, NDEV, stride=2), :]
    blocks = C // GW
    packed = pack[...].reshape(NDEV, 8, half).astype(BF16)
    gg = taps[...].T.reshape(blocks, GW, C).astype(BF16)
    for at, plane in enumerate(ORDER):
        for part in range(NDEV // blocks):
            pay[at, :, part * half : (part + 1) * half] = packed[part * blocks + plane]
        pay[at, :, 4 * half :] = gg[plane]


def own_dx_kernel(own, cot, w_in, dx):
    dx[...] = (cot[...].astype(F32) + dot_nt(own[...], w_in[...])).astype(BF16)


def pair_dx_kernel(near, far, w_in, dx_near, dx_far):
    dx_near[...] = dot_nt(near[...], w_in[...]).astype(BF16)
    dx_far[...] = dot_nt(far[...], w_in[...]).astype(BF16)


def first_sum_kernel(got, pay):
    total = jnp.sum(got[...].astype(F32), axis=0)
    half = C // 2
    for at, part in enumerate(SAMPLE_ORDER):
        pay[at, :, 0:half] = total[:, part * half : (part + 1) * half]
        pay[at, :, half:] = total[:, 4 * half :]


def sum_kernel(got, dx, dxl, dxr, grad_in, grad_out, gg, section):
    section[...] = (
        dx[...].astype(F32) + (dxl[...].astype(F32) + dxr[...].astype(F32))
    ).astype(BF16)
    total = jnp.sum(got[...].astype(F32), axis=0)
    half = C // 2
    for which, out in enumerate((grad_in, grad_out)):
        for parity in range(2):
            for side in range(2):
                row = which * 4 + parity * 2 + side
                out[parity : parity + 1, side * half : (side + 1) * half] = total[
                    row : row + 1, 0:half
                ]
    gg[...] = total[:, half:].T[0 : TAPS * GW, :]


def call(kernel, outs, scratch, flops, *args, space=pltpu.VMEM):
    shapes = [jax.ShapeDtypeStruct(shape, dtype) for shape, dtype in outs]
    size = sum(a.size * a.dtype.itemsize for a in (*args, *shapes))
    return pl.pallas_call(
        kernel,
        out_shape=shapes,
        in_specs=[pl.BlockSpec(memory_space=space)] * len(args),
        out_specs=[pl.BlockSpec(memory_space=pltpu.VMEM)] * len(outs),
        scratch_shapes=[
            pltpu.VMEM(*entry) if isinstance(entry, tuple) else entry for entry in scratch
        ],
        cost_estimate=pl.CostEstimate(flops=flops, bytes_accessed=size, transcendentals=0),
        compiler_params=pltpu.CompilerParams(vmem_limit_bytes=8 * 1024 * 1024),
        interpret=INTERPRET,
    )(*args)


PLANE = (CELLS, C)
BUF = ((PAD_ROWS, 3 * C), BF16)
PAY = (C // GW, 8, 3 * C)
TILE = 2 * C**3


def own_stage(x, cot, w_in, w_out, wg):
    return call(
        own_kernel,
        [(PLANE, F32), (PLANE, BF16), (PLANE, BF16), ((TAPS * C, C), BF16), (PLANE, F32)]
        + [(PLANE, BF16)] * 3,
        [(PLANE, BF16), ((PAD_ROWS, C), BF16), (PLANE, BF16), ((TAPS * GW, C), BF16), pltpu.SemaphoreType.DMA((5,))],
        11 * TILE,
        x, cot, w_in, w_out, wg,
        space=pltpu.HBM,
    )


def far_stage(*args):
    return call(
        far_kernel, [(PLANE, BF16), (PLANE, F32), (PLANE, F32), (PLANE, BF16)], [((PAD_ROWS, C), BF16)], 10 * TILE, *args
    )


def middle_stage(*args):
    return call(
        middle_kernel,
        [(PLANE, BF16)] * 3 + [(PAY, BF16)],
        [
            ((PAD_ROWS, C), BF16),
            BUF,
            ((2, 3 * C // 2, CELLS), BF16),
            (PLANE, F32),
            (PLANE, F32),
            ((4, C, C // 2), F32),
            ((NDEV * 8, C // 2), F32),
        ],
        70 * TILE,
        *args,
    )


def own_dx_stage(*args):
    return call(own_dx_kernel, [(PLANE, BF16)], [], TILE, *args)[0]


def pair_dx_stage(*args):
    return call(pair_dx_kernel, [(PLANE, BF16)] * 2, [], 2 * TILE, *args)


def first_sum_stage(got):
    return call(first_sum_kernel, [((4, 8, 3 * C // 2), F32)], [], 1000, got)[0]


def sum_stage(*args):
    return call(
        sum_kernel,
        [((2, C), F32), ((2, C), F32), ((TAPS * GW, GW), F32), (PLANE, BF16)],
        [],
        1000,
        *args,
    )


def near_of(plane):
    return plane ^ 1


def far_of(plane):
    return plane - 1 if plane % 2 == 0 else plane + 1


def sent(value, back, partner):
    pipes, planes = lax.axis_size("pipe"), lax.axis_size("sg")
    pairs = [
        (pipe * planes + plane, (pipe - back) * planes + partner(plane))
        for pipe in range(back, pipes)
        for plane in range(planes)
        if 0 <= partner(plane) < planes
    ]
    return lax.ppermute(value, ("pipe", "sg"), pairs)


def per_device(inputs, cotangent, w_in, w_out, w_group):
    shape = inputs.shape
    x = inputs.reshape(PLANE)
    cot = cotangent.reshape(PLANE)
    w_in = w_in.reshape(C, C)
    w_out = w_out.reshape(C, C)
    wg = w_group.reshape(TAPS * GW, C)
    far = sent(x, 0, far_of)
    near = sent(x, 0, near_of)
    kept = [
        pltpu.with_memory_space_constraint(value, pltpu.HBM)
        for value in (x, cot, w_in, w_out, wg)
    ]
    slope1, h1t, dh2, wd, z2p, xt, cot, w_in = own_stage(*kept)
    h1ft, slopef, z2f, far_t = far_stage(far, w_in, wd, z2p)
    own, to_near, to_far, pay = middle_stage(
        near, far_t, xt, cot, w_in, wd, z2f, dh2, h1t, slope1, h1ft, slopef
    )
    dx = own_dx_stage(own, cot, w_in)
    part = first_sum_stage(lax.all_to_all(pay, "sg", 0, 0, tiled=True, axis_index_groups=[ORDER]))
    got = lax.all_to_all(
        part, "dp", 0, 0, tiled=True, axis_index_groups=[SAMPLE_ORDER]
    )
    dx_near, dx_far = pair_dx_stage(to_near, to_far, w_in)
    dx = sent(dx, 1, lambda plane: plane)
    dx_far = sent(dx_far, 1, far_of)
    dx_near = sent(dx_near, 1, near_of)
    grad_in, grad_out, gg, section_grad = sum_stage(got, dx, dx_near, dx_far)
    return (
        section_grad.reshape(shape),
        grad_in[None],
        grad_out[None],
        gg.reshape(1, 3, 3, 3, GW, GW),
    )


def solution(mesh):
    placed = (
        P("pipe", "dp", "sg", None, None, None),
        P("pipe", "dp", "sg", None, None, None),
        P("pipe", None, None),
        P("pipe", None, None),
        P("pipe", None, None, None, None, None),
    )
    return jax.shard_map(
        per_device,
        mesh=mesh,
        in_specs=placed,
        out_specs=(
            P("pipe", "dp", "sg", None, None, None),
            P("pipe", ("dp", "sg"), None),
            P("pipe", ("dp", "sg"), None),
            P("pipe", None, None, None, None, "sg"),
        ),
        check_vma=False,
    )
```

```python
import functools

import jax
import jax.numpy as jnp
from jax import lax
from jax.experimental import pallas as pl
from jax.experimental.pallas import tpu as pltpu
from jax.sharding import PartitionSpec as P

F32 = jnp.float32
BF16 = jnp.bfloat16

C = 256
GW = 8
SIDE = 16
CELLS = SIDE * SIDE
TAPS = 27
PAD_ROWS = CELLS + 2 * SIDE
NDEV = 128
INTERPRET = False
SAMPLE_ORDER = [2, 3, 0, 1]
ORDER = [(20 - step) % (C // GW) for step in range(C // GW)]

NT = (((1,), (1,)), ((), ()))


def dot(a, b):
    return jnp.dot(a, b, preferred_element_type=F32)


def dot_nt(a, b):
    return lax.dot_general(a, b, NT, preferred_element_type=F32)


def sigmoid(v):
    return 1.0 / (1.0 + jnp.exp(-v))


def column():
    return lax.broadcasted_iota(jnp.int32, (CELLS, C), 0) % SIDE


def fill(buf, plane, sign):
    zeros = jnp.zeros((SIDE, 3 * C), BF16)
    buf[0:SIDE, :] = zeros
    buf[SIDE + CELLS :, :] = zeros
    col = column()
    ahead = jnp.where(col < SIDE - 1, pltpu.roll(plane, CELLS - 1, 0), 0.0)
    behind = jnp.where(col > 0, pltpu.roll(plane, 1, 0), 0.0)
    left, right = (behind, ahead) if sign > 0 else (ahead, behind)
    buf[SIDE : SIDE + CELLS, 0:C] = left.astype(BF16)
    buf[SIDE : SIDE + CELLS, C : 2 * C] = plane.astype(BF16)
    buf[SIDE : SIDE + CELLS, 2 * C :] = right.astype(BF16)


def conv_shifted(rows, wd, depth):
    sums = []
    for col in range(3):
        total = None
        for row in range(3):
            term = dot(rows[row * SIDE : row * SIDE + CELLS, :], wd[pl.ds(tap(depth, row, col), C), :])
            total = term if total is None else total + term
        sums.append(total)
    at = column()
    behind = jnp.where(at > 0, pltpu.roll(sums[0], 1, 0), 0.0)
    ahead = jnp.where(at < SIDE - 1, pltpu.roll(sums[2], CELLS - 1, 0), 0.0)
    return sums[1] + (behind + ahead)


def keep_rows(rows, plane):
    zeros = jnp.zeros((SIDE, C), BF16)
    rows[0:SIDE, :] = zeros
    rows[SIDE : SIDE + CELLS, :] = plane
    rows[SIDE + CELLS :, :] = zeros


def tap(depth, row, col=0):
    start = ((depth * 3 + row) * 3 + col) * C
    return start if isinstance(start, int) else pl.multiple_of(start, C)


def conv_plane(buf, wd, depth):
    total = None
    for row in range(3):
        term = dot(buf[row * SIDE : row * SIDE + CELLS, :], wd[pl.ds(tap(depth, row), 3 * C), :])
        total = term if total is None else total + term
    return total


def conv_plane_back(buf, wd, depth):
    total = None
    for row in range(3):
        for col in range(3):
            rows = (2 - row) * SIDE
            term = dot_nt(
                buf[rows : rows + CELLS, col * C : (col + 1) * C],
                wd[pl.ds(tap(depth, row, col), C), :],
            )
            total = term if total is None else total + term
    return total


def neighbour_depths():
    odd = lax.axis_index("sg") % 2
    return 2 - 2 * odd, 2 * odd


def activate(x, w_in):
    z1 = dot(x[...], w_in[...])
    sig = sigmoid(z1)
    return (z1 * sig).astype(BF16), sig * (1.0 + z1 * (1.0 - sig))


def far_kernel(far, w_in, wd, z2p, h1t, slope, total, far_t, buf):
    act, grad = activate(far, w_in)
    slope[...] = grad
    h1t[...] = act.T
    far_t[...] = far[...].T
    keep_rows(buf, act)
    total[...] = z2p[...] + conv_shifted(buf, wd, neighbour_depths()[1])


def spread(wg, wd, which):
    same = (
        lax.broadcasted_iota(jnp.int32, (C, C), 0) // GW
        == lax.broadcasted_iota(jnp.int32, (C, C), 1) // GW
    )
    taps = wg[...].astype(F32)
    for k in which:
        rows = jnp.broadcast_to(taps[k * GW : (k + 1) * GW, :][None], (C // GW, GW, C))
        wd[k * C : (k + 1) * C, :] = jnp.where(same, rows.reshape(C, C), 0.0).astype(BF16)


def own_kernel(
    x_hbm, cot_hbm, w_in_hbm, w_out_hbm, wg_hbm,
    slope1, h1t, dh2, wd, z2p, xt, cot, w_in,
    x, buf, w_out, wg, sems,
):
    copies = [
        pltpu.make_async_copy(source, target, sems.at[i])
        for i, (source, target) in enumerate(
            ((wg_hbm, wg), (x_hbm, x), (w_in_hbm, w_in), (cot_hbm, cot), (w_out_hbm, w_out))
        )
    ]
    for copy in copies:
        copy.start()
    copies[0].wait()
    spread(wg, wd, range(TAPS))
    for copy in copies[1:]:
        copy.wait()
    act, grad = activate(x, w_in)
    slope1[...] = grad
    h1t[...] = act.T
    xt[...] = x[...].T
    dh2[...] = dot_nt(cot[...], w_out[...]).astype(BF16)
    keep_rows(buf, act)
    z2p[...] = conv_shifted(buf, wd, 1)


def middle_kernel(
    near, far_t, xt, cot, w_in, wd, z2f, dh2, h1t, slope1, h1ft, slopef,
    own, to_near, to_far, pay,
    bufn, buf, ht, slopen, taps, grads, pack,
):
    half = C // 2
    depth_near, depth_far = neighbour_depths()
    act, grad = activate(near, w_in)
    slopen[...] = grad
    keep_rows(bufn, act)
    total = z2f[...] + conv_shifted(bufn, wd, depth_near)
    sig = sigmoid(total)
    h2 = (total * sig).astype(BF16)
    slope = sig * (1.0 + total * (1.0 - sig))
    back = (dh2[...].astype(F32) * slope).astype(BF16)
    fill(buf, back.astype(F32), -1)
    outer = dot(h2.T, cot[...])
    for side in range(2):
        grads[2 + side] = outer[:, side * half : (side + 1) * half]
    share = (conv_plane_back(buf, wd, 1) * slope1[...]).astype(BF16)
    own[...] = share
    outer = dot(xt[...], share)
    for turned, out, slope, depth in (
        (far_t[...], to_far, slopef, depth_far),
        (near[...].T, to_near, slopen, depth_near),
    ):
        share = (conv_plane_back(buf, wd, depth) * slope[...]).astype(BF16)
        outer = outer + dot(turned, share)
        out[...] = share
    for side in range(2):
        grads[side] = outer[:, side * half : (side + 1) * half]
    for which, turned in enumerate((h1ft[...], h1t[...], act.T)):
        for side in range(2):
            ht[side, which * half : (which + 1) * half, :] = turned[
                side * half : (side + 1) * half, :
            ]
    groups = half // GW
    same = (
        lax.broadcasted_iota(jnp.int32, (half, half), 0) // GW
        == lax.broadcasted_iota(jnp.int32, (half, half), 1) // GW
    )
    taps[TAPS * GW :, :] = jnp.zeros((C - TAPS * GW, C), F32)
    for row in range(3):
        rows = (2 - row) * SIDE
        for side in range(2):
            wide = jnp.concatenate(
                [
                    buf[rows : rows + CELLS, col * C + side * half : col * C + (side + 1) * half]
                    for col in range(3)
                ],
                axis=1,
            )
            full = dot(ht[side], wide)
            for col in range(3):
                for which, depth in enumerate((depth_far, 1, depth_near)):
                    block = jnp.where(
                        same,
                        full[which * half : (which + 1) * half, col * half : (col + 1) * half],
                        0.0,
                    )
                    first = ((depth * 3 + row) * 3 + col) * GW
                    taps[pl.ds(first, GW), side * half : (side + 1) * half] = jnp.sum(
                        block.reshape(groups, GW, half), axis=0
                    )
    for which in range(2):
        for parity in range(2):
            for side in range(2):
                pack[pl.ds(which * 4 + parity * 2 + side, NDEV, stride=8), :] = grads.at[
                    which * 2 + side
                ][pl.ds(parity, NDEV, stride=2), :]
    blocks = C // GW
    packed = pack[...].reshape(NDEV, 8, half).astype(BF16)
    gg = taps[...].T.reshape(blocks, GW, C).astype(BF16)
    for at, plane in enumerate(ORDER):
        for part in range(NDEV // blocks):
            pay[at, :, part * half : (part + 1) * half] = packed[part * blocks + plane]
        pay[at, :, 4 * half :] = gg[plane]


def own_dx_kernel(own, cot, w_in, dx):
    dx[...] = (cot[...].astype(F32) + dot_nt(own[...], w_in[...])).astype(BF16)


def pair_dx_kernel(near, far, w_in, dx_near, dx_far):
    dx_near[...] = dot_nt(near[...], w_in[...]).astype(BF16)
    dx_far[...] = dot_nt(far[...], w_in[...]).astype(BF16)


def first_sum_kernel(got, pay):
    total = jnp.sum(got[...].astype(F32), axis=0)
    half = C // 2
    for at, part in enumerate(SAMPLE_ORDER):
        pay[at, :, 0:half] = total[:, part * half : (part + 1) * half]
        pay[at, :, half:] = total[:, 4 * half :]


def section_kernel(dx, dx_near, dx_far, section):
    section[...] = (
        dx[...].astype(F32) + (dx_near[...].astype(F32) + dx_far[...].astype(F32))
    ).astype(BF16)


def sum_kernel(got, grad_in, grad_out, gg):
    total = jnp.sum(got[...].astype(F32), axis=0)
    half = C // 2
    for which, out in enumerate((grad_in, grad_out)):
        for parity in range(2):
            for side in range(2):
                row = which * 4 + parity * 2 + side
                out[parity : parity + 1, side * half : (side + 1) * half] = total[
                    row : row + 1, 0:half
                ]
    gg[...] = total[:, half:].T[0 : TAPS * GW, :]


def call(kernel, outs, scratch, flops, *args, space=pltpu.VMEM):
    shapes = [jax.ShapeDtypeStruct(shape, dtype) for shape, dtype in outs]
    size = sum(a.size * a.dtype.itemsize for a in (*args, *shapes))
    return pl.pallas_call(
        kernel,
        out_shape=shapes,
        in_specs=[pl.BlockSpec(memory_space=space)] * len(args),
        out_specs=[pl.BlockSpec(memory_space=pltpu.VMEM)] * len(outs),
        scratch_shapes=[
            pltpu.VMEM(*entry) if isinstance(entry, tuple) else entry for entry in scratch
        ],
        cost_estimate=pl.CostEstimate(flops=flops, bytes_accessed=size, transcendentals=0),
        compiler_params=pltpu.CompilerParams(vmem_limit_bytes=8 * 1024 * 1024),
        interpret=INTERPRET,
    )(*args)


PLANE = (CELLS, C)
BUF = ((PAD_ROWS, 3 * C), BF16)
PAY = (C // GW, 8, 3 * C)
TILE = 2 * C**3


def own_stage(x, cot, w_in, w_out, wg):
    return call(
        own_kernel,
        [(PLANE, F32), (PLANE, BF16), (PLANE, BF16), ((TAPS * C, C), BF16), (PLANE, F32)]
        + [(PLANE, BF16)] * 3,
        [(PLANE, BF16), ((PAD_ROWS, C), BF16), (PLANE, BF16), ((TAPS * GW, C), BF16), pltpu.SemaphoreType.DMA((5,))],
        11 * TILE,
        x, cot, w_in, w_out, wg,
        space=pltpu.HBM,
    )


def far_stage(*args):
    return call(
        far_kernel, [(PLANE, BF16), (PLANE, F32), (PLANE, F32), (PLANE, BF16)], [((PAD_ROWS, C), BF16)], 10 * TILE, *args
    )


def middle_stage(*args):
    return call(
        middle_kernel,
        [(PLANE, BF16)] * 3 + [(PAY, BF16)],
        [
            ((PAD_ROWS, C), BF16),
            BUF,
            ((2, 3 * C // 2, CELLS), BF16),
            (PLANE, F32),
            (PLANE, F32),
            ((4, C, C // 2), F32),
            ((NDEV * 8, C // 2), F32),
        ],
        70 * TILE,
        *args,
    )


def own_dx_stage(*args):
    return call(own_dx_kernel, [(PLANE, BF16)], [], TILE, *args)[0]


def pair_dx_stage(*args):
    return call(pair_dx_kernel, [(PLANE, BF16)] * 2, [], 2 * TILE, *args)


def first_sum_stage(got):
    return call(first_sum_kernel, [((4, 8, 3 * C // 2), F32)], [], 1000, got)[0]


def section_stage(*args):
    return call(section_kernel, [(PLANE, BF16)], [], 1000, *args)[0]


def sum_stage(*args):
    return call(
        sum_kernel,
        [((2, C), F32), ((2, C), F32), ((TAPS * GW, GW), F32)],
        [],
        1000,
        *args,
    )


def near_of(plane):
    return plane ^ 1


def far_of(plane):
    return plane - 1 if plane % 2 == 0 else plane + 1


def sent(value, back, partner):
    pipes, planes = lax.axis_size("pipe"), lax.axis_size("sg")
    pairs = [
        (pipe * planes + plane, (pipe - back) * planes + partner(plane))
        for pipe in range(back, pipes)
        for plane in range(planes)
        if 0 <= partner(plane) < planes
    ]
    return lax.ppermute(value, ("pipe", "sg"), pairs)


def per_device(inputs, cotangent, w_in, w_out, w_group):
    shape = inputs.shape
    x = inputs.reshape(PLANE)
    cot = cotangent.reshape(PLANE)
    w_in = w_in.reshape(C, C)
    w_out = w_out.reshape(C, C)
    wg = w_group.reshape(TAPS * GW, C)
    far = sent(x, 0, far_of)
    near = sent(x, 0, near_of)
    kept = [
        pltpu.with_memory_space_constraint(value, pltpu.HBM)
        for value in (x, cot, w_in, w_out, wg)
    ]
    slope1, h1t, dh2, wd, z2p, xt, cot, w_in = own_stage(*kept)
    h1ft, slopef, z2f, far_t = far_stage(far, w_in, wd, z2p)
    own, to_near, to_far, pay = middle_stage(
        near, far_t, xt, cot, w_in, wd, z2f, dh2, h1t, slope1, h1ft, slopef
    )
    dx = own_dx_stage(own, cot, w_in)
    part = first_sum_stage(lax.all_to_all(pay, "sg", 0, 0, tiled=True, axis_index_groups=[ORDER]))
    got = lax.all_to_all(
        part, "dp", 0, 0, tiled=True, axis_index_groups=[SAMPLE_ORDER]
    )
    dx_near, dx_far = pair_dx_stage(to_near, to_far, w_in)
    dx = sent(dx, 1, lambda plane: plane)
    dx_far = sent(dx_far, 1, far_of)
    dx_near = sent(dx_near, 1, near_of)
    section_grad = section_stage(dx, dx_near, dx_far)
    grad_in, grad_out, gg = sum_stage(got)
    return (
        section_grad.reshape(shape),
        grad_in[None],
        grad_out[None],
        gg.reshape(1, 3, 3, 3, GW, GW),
    )


def solution(mesh):
    placed = (
        P("pipe", "dp", "sg", None, None, None),
        P("pipe", "dp", "sg", None, None, None),
        P("pipe", None, None),
        P("pipe", None, None),
        P("pipe", None, None, None, None, None),
    )
    return jax.shard_map(
        per_device,
        mesh=mesh,
        in_specs=placed,
        out_specs=(
            P("pipe", "dp", "sg", None, None, None),
            P("pipe", ("dp", "sg"), None),
            P("pipe", ("dp", "sg"), None),
            P("pipe", None, None, None, None, "sg"),
        ),
        check_vma=False,
    )
```
